512 devices in a mesh: sample: 32 (over y, x, core), space: 16 (over z).
Axes of the slice: x: 4, y: 4, z: 16, core: 2. Of those that a mesh axis runs over, the one named last changes fastest.
Arguments:
- volumes: bfloat16 [32, 32, 64, 16, 128], P('sample', None, 'space'), may hold values from -360 to 360
- depth_kernel: float32 [32, 27], replicated, may hold values from -1.25 to 1.25
- point_weight: bfloat16 [32, 32], replicated, may hold values from -1 to 1
- cotangent: bfloat16 [32, 32, 64, 16, 128], P('sample', None, 'space'), may hold values from -4.1 to 4.1
Outputs:
- whitened: bfloat16 [32, 32, 64, 16, 128], P('sample', None, 'space')
- d_volumes: bfloat16 [32, 32, 64, 16, 128], P('sample', None, 'space')
- d_point: float32 [32, 32], replicated
- d_kernel: float32 [32, 27], replicated
The draws below stay inside these ranges and needn't reach their ends.
All inputs are finite; a program needn't handle non-finite values.
Results may differ from the reference program's by a relative error of at most 0.0067.
Values may be sent and summed in bfloat16 or wider, within the bound.
No kernel may reach another device: no remote copies, remote signals or barrier semaphores. Data moves between devices by JAX's collectives and lax.ppermute only.
A program may use at most 64 MiB of HBM per device.

```python
import math
from functools import partial
import jax
import jax.numpy as jnp
from jax import lax

C = 32
GSIZE = 16
NEWTON = 5
HY = 16
WX = 128
GROUPS = 2
VOLUMES = 32
NZ = 64
COUNT = 4194304


def draw_volumes(key, part):
    keys = jax.random.split(key, 7)
    shape_all = (VOLUMES, C, NZ, HY, WX)
    channel_scale = jnp.exp(jax.random.uniform(keys[0], (C,), jnp.float32) * math.log(10.0))
    order = jax.random.permutation(keys[1], VOLUMES).astype(jnp.float32)
    volume_scale = jnp.exp(order / max(VOLUMES - 1, 1) * math.log(3.0))
    depth_scale = jnp.exp(jax.random.uniform(keys[2], (VOLUMES, NZ), jnp.float32) * math.log(2.0))
    shared_mix = jax.random.uniform(keys[3], (C,), jnp.float32, -1.0, 1.0)
    own_mix = jax.random.uniform(keys[4], (VOLUMES, C), jnp.float32, -1.0, 1.0)
    scales = volume_scale[:, None, None, None, None] * channel_scale[None, :, None, None, None] * depth_scale[:, None, :, None, None]
    mixing = 0.6 * shared_mix[None, :] + 0.4 * own_mix
    base_values = jax.random.truncated_normal(keys[5], -3.0, 3.0, shape_all, jnp.float32)
    common = jax.random.truncated_normal(keys[6], -3.0, 3.0, (VOLUMES, 1, NZ, HY, WX), jnp.float32)
    core = base_values + mixing[:, :, None, None, None] * common
    return (core * scales).astype(jnp.bfloat16)


def draw_cotangent(key, part):
    keys = jax.random.split(jax.random.fold_in(key, 17), 3)
    shape_all = (VOLUMES, C, NZ, HY, WX)
    shift = 0.4 * jax.random.uniform(keys[0], (C,), jnp.float32, -1.0, 1.0)[None, :] + 0.15 * jax.random.uniform(keys[1], (VOLUMES, C), jnp.float32, -1.0, 1.0)
    noise = jax.random.truncated_normal(keys[2], -3.5, 3.5, shape_all, jnp.float32)
    return (noise + shift[:, :, None, None, None]).astype(jnp.bfloat16)


def scatter_about(stream_key, dims, deviation, reach, kind=jnp.bfloat16):
    entries = jax.random.normal(stream_key, dims, jnp.float32) * deviation
    return jnp.minimum(jnp.maximum(entries, -reach), reach).astype(kind)


def setup_inputs(seed: int = 0) -> dict:
    arg_keys = jax.random.split(jax.random.key(seed), 5)
    return {
        "volumes": draw_volumes(jax.random.fold_in(arg_keys[4], 71), 0),
        "depth_kernel": scatter_about(arg_keys[1], (C, 27), 27 ** -0.5, 1.25, jnp.float32),
        "point_weight": scatter_about(arg_keys[2], (C, C), C ** -0.5, 1.0),
        "cotangent": draw_cotangent(jax.random.fold_in(arg_keys[4], 71), 0),
    }


epsilon = 1e-05
highest = lax.Precision.HIGHEST

def matmul_high(matrix, operand):
    return jnp.matmul(matrix, operand, precision=highest)

def contract_rows(matrix, operand):
    return jnp.einsum('cv,dv->cd', matrix, operand, precision=highest, preferred_element_type=jnp.float32)

def contract_cols(matrix, operand):
    return jnp.einsum('kc,kv->cv', matrix, operand, precision=highest, preferred_element_type=jnp.float32)

def block_diagonal(blocks):
    identity = jnp.eye(blocks.shape[0], dtype=blocks.dtype)
    full_size = blocks.shape[0] * blocks.shape[1]
    return jnp.einsum('gh,gij->gihj', identity, blocks, precision=highest).reshape(full_size, full_size)

def whiten_stats(first_sums, second_sums, voxel_count):
    groups = second_sums.shape[0]
    group_size = second_sums.shape[1]
    average = (first_sums / voxel_count).reshape(groups, group_size)
    identity = jnp.eye(group_size, dtype=second_sums.dtype)
    covariance = second_sums / voxel_count - average[:, :, None] * average[:, None, :] + epsilon * identity
    traces = jnp.trace(covariance, axis1=1, axis2=2)
    normed = covariance / traces[:, None, None]
    project = jnp.broadcast_to(identity, covariance.shape)
    for newton_step in range(NEWTON):
        cubed = matmul_high(matmul_high(project, project), project)
        project = 0.5 * (3.0 * project - matmul_high(cubed, normed))
    whiten_mat = project / jnp.sqrt(traces)[:, None, None]
    offset = jnp.einsum('gij,gj->gi', whiten_mat, average, precision=highest)
    return (whiten_mat, offset)

def adjoint_terms(pull_back, whiten_mat, grad_first, grad_second):
    d_first, d_second = pull_back((grad_second, -grad_first.reshape(whiten_mat.shape[0], whiten_mat.shape[1])))
    adjoint = block_diagonal(jnp.swapaxes(whiten_mat, 1, 2))
    symmetric = block_diagonal(d_second + jnp.swapaxes(d_second, 1, 2))
    return (d_first, adjoint, symmetric)

def gradient_signal(adjoint, d_first, symmetric, grad_part, mixed_part):
    first_term = jnp.dot(adjoint, grad_part, precision=highest, preferred_element_type=jnp.float32)
    third_term = jnp.dot(symmetric, mixed_part, precision=highest, preferred_element_type=jnp.float32)
    return first_term + d_first[:, None] + third_term

def pad_sides(extended):
    return jnp.pad(extended, ((0, 0), (0, 0), (1, 1), (1, 1)))

def tap_cells(padded, tap_index, depth_cells):
    plane_off = tap_index // 9
    row_off = tap_index // 3 % 3
    col_off = tap_index % 3
    height = padded.shape[2] - 2
    width_cells = padded.shape[3] - 2
    return padded[:, plane_off:plane_off + depth_cells, row_off:row_off + height, col_off:col_off + width_cells]

def depth_conv(extended, kernel, depth_cells):
    padded = pad_sides(extended)
    summed = jnp.zeros((extended.shape[0], depth_cells, extended.shape[2], extended.shape[3]), jnp.float32)
    for tap_index in range(27):
        summed = summed + kernel[:, tap_index][:, None, None, None] * tap_cells(padded, tap_index, depth_cells).astype(jnp.float32)
    return summed

def depth_adjoint(grad_ext, kernel, depth_cells):
    padded = pad_sides(grad_ext)
    height = grad_ext.shape[2]
    width_cells = grad_ext.shape[3]
    summed = jnp.zeros((grad_ext.shape[0], depth_cells, height, width_cells), jnp.float32)
    for tap_index in range(27):
        plane_off = 2 - tap_index // 9
        row_off = 2 - tap_index // 3 % 3
        col_off = 2 - tap_index % 3
        summed = summed + kernel[:, tap_index][:, None, None, None] * padded[:, plane_off:plane_off + depth_cells, row_off:row_off + height, col_off:col_off + width_cells]
    return summed

def forward_volume(volume, depth_kernel, point_weight):
    extended = jnp.pad(volume, ((0, 0), (1, 1), (0, 0), (0, 0)))
    hidden = depth_conv(extended, depth_kernel, NZ).astype(jnp.bfloat16).reshape(C, -1)
    mixed_out = jnp.dot(point_weight, hidden, preferred_element_type=jnp.float32).astype(jnp.bfloat16)
    return (extended, hidden, mixed_out)

def reference(volumes, depth_kernel, point_weight, cotangent):
    voxel_count = float(COUNT)

    def stat_step(running, volume):
        mixed_out = forward_volume(volume, depth_kernel, point_weight)[2]
        grouped = mixed_out.reshape(GROUPS, GSIZE, -1).astype(jnp.float32)
        first_new = running[0] + lax.optimization_barrier(jnp.sum(grouped, axis=2)).reshape(C)
        second_new = running[1] + jnp.einsum('giv,gjv->gij', grouped, grouped)
        return ((first_new, second_new), None)
    zero_sums = (jnp.zeros((C,), jnp.float32), jnp.zeros((GROUPS, GSIZE, GSIZE), jnp.float32))
    (first_sums, second_sums), ignored = lax.scan(stat_step, zero_sums, volumes)
    (whiten_mat, offset), pull_back = jax.vjp(partial(whiten_stats, voxel_count=voxel_count), first_sums, second_sums)
    full_white = block_diagonal(whiten_mat)

    def white_step(running, volume_pair):
        volume, grad_in = volume_pair
        mixed_out = forward_volume(volume, depth_kernel, point_weight)[2]
        whitened = (jnp.dot(full_white, mixed_out, precision=highest, preferred_element_type=jnp.float32) - offset.reshape(C)[:, None]).astype(jnp.bfloat16)
        grad_flat = grad_in.reshape(C, -1).astype(jnp.float32)
        grouped = mixed_out.reshape(GROUPS, GSIZE, -1).astype(jnp.float32)
        first_new = running[0] + lax.optimization_barrier(jnp.sum(grad_flat, axis=1))
        second_new = running[1] + jnp.einsum('giv,gjv->gij', grad_flat.reshape(GROUPS, GSIZE, -1), grouped)
        return ((first_new, second_new), whitened.reshape(C, NZ, HY, WX))
    (grad_first, grad_second), whitened_all = lax.scan(white_step, zero_sums, (volumes, cotangent))
    d_first, adjoint, symmetric = adjoint_terms(pull_back, whiten_mat, grad_first, grad_second)
    weight_f = point_weight.astype(jnp.float32)

    def grad_step(running, volume_pair):
        volume, grad_in = volume_pair
        extended, hidden, mixed_out = forward_volume(volume, depth_kernel, point_weight)
        d_mixed = gradient_signal(adjoint, d_first, symmetric, grad_in.reshape(C, -1), mixed_out)
        d_hidden = contract_cols(weight_f, d_mixed).reshape(C, NZ, HY, WX)
        padded_x = pad_sides(extended)
        kernel_terms = jnp.stack([lax.optimization_barrier(jnp.sum(d_hidden * tap_cells(padded_x, tap_index, NZ).astype(jnp.float32), axis=(1, 2, 3))) for tap_index in range(27)], axis=1)
        grad_ext = jnp.pad(d_hidden, ((0, 0), (1, 1), (0, 0), (0, 0)))
        d_volume = depth_adjoint(grad_ext, depth_kernel, NZ).astype(jnp.bfloat16)
        return ((running[0] + contract_rows(d_mixed, hidden), running[1] + kernel_terms), d_volume)
    zero_grads = (jnp.zeros((C, C), jnp.float32), jnp.zeros((C, 27), jnp.float32))
    (d_point, d_kernel), d_volumes = lax.scan(grad_step, zero_grads, (volumes, cotangent))
    scale_out = 1.0 / math.sqrt(voxel_count)
    return (whitened_all, d_volumes, d_point * scale_out, d_kernel * scale_out)
```

```python
import math

import jax
import jax.numpy as jnp
from jax import lax
from jax.experimental import pallas as pl
from jax.experimental.pallas import tpu as pltpu
from jax.sharding import PartitionSpec as P

NEWTON = 5
EPSILON = 1e-05
C = 32
D = 4
H = 16
W = 128
HW = H * W
PW = (H + 2) * W
ROWS = 24
HIGH = lax.Precision.HIGHEST
F32 = jnp.float32
BF16 = jnp.bfloat16


def dot(a, b, dims=((1,), (0,)), precision=None):
    return lax.dot_general(
        a, b, (dims, ((), ())), precision=precision, preferred_element_type=F32
    )


def dot_high(a, b, dims=((1,), (0,))):
    return dot(a, b, dims, HIGH)


def iota(shape, dim):
    return lax.broadcasted_iota(jnp.int32, shape, dim)


def spread_taps(dk_ref, taps_ref, flip):
    for t in range(27):
        s = 26 - t if flip else t
        taps_ref[t] = jnp.broadcast_to(dk_ref[:, s : s + 1], (C, W))


def stencil(src_ref, taps_ref, dst_ref, planes):
    lane = iota((8, W), 1)
    for group in range(C // 8):
        rows = pl.ds(8 * group, 8)
        taps = [taps_ref[t, rows, :] for t in range(27)]

        def plane(p, carry):
            for h in range(H):
                parts = [None, None, None]
                for a in range(3):
                    for b in range(3):
                        cells = src_ref[p + a, rows, (h + b) * W : (h + b + 1) * W]
                        for e in range(3):
                            term = taps[9 * a + 3 * b + e] * cells
                            parts[e] = term if parts[e] is None else parts[e] + term
                left = jnp.where(lane == 0, 0.0, pltpu.roll(parts[0], 1, 1))
                right = jnp.where(lane == W - 1, 0.0, pltpu.roll(parts[2], W - 1, 1))
                dst_ref[p, rows, h * W : (h + 1) * W] = parts[1] + left + right
            return carry

        lax.fori_loop(0, planes, plane, 0)


def sums_kernel(x_ref, g_ref, lo_ref, hi_ref, dk_ref, w_ref, gm_ref, send_ref,
                xf_ref, xb_ref, hid_ref, taps_ref, right_ref, acc_ref):
    zeros = jnp.zeros((D + 4, C, W), F32)
    xf_ref[:, :, 0:W] = zeros
    xf_ref[:, :, PW - W : PW] = zeros
    xb_ref[:, :, 0:W] = zeros[: D + 2].astype(BF16)
    xb_ref[:, :, PW - W : PW] = zeros[: D + 2].astype(BF16)
    for p in range(D + 4):
        if p < 2:
            cells = lo_ref[:, p]
        elif p < D + 2:
            cells = x_ref[:, p - 2]
        else:
            cells = hi_ref[:, p - D - 2]
        cells = cells.reshape(C, HW)
        xf_ref[p, :, W : W + HW] = cells.astype(F32)
        if 1 <= p <= D + 2:
            xb_ref[p - 1, :, W : W + HW] = cells
    for p in range(D + 2):
        if p == 0:
            cells = lo_ref[:, 2]
        elif p <= D:
            cells = g_ref[:, p - 1]
        else:
            cells = hi_ref[:, 2]
        gm_ref[p, 0:C, :] = cells.reshape(C, HW)
    spread_taps(dk_ref, taps_ref, False)
    stencil(xf_ref, taps_ref, hid_ref, D + 2)

    def mix(p, carry):
        hidden = hid_ref[p].astype(BF16)
        gm_ref[p, C : 2 * C, :] = dot(w_ref[...], hidden).astype(BF16)
        return carry

    lax.fori_loop(0, D + 2, mix, 0)

    lane = iota((1, W), 1)
    row16 = iota((16, W), 0)
    lane16 = iota((16, W), 1)
    keep0 = (lane < W - 1).astype(F32).astype(BF16)
    keep2 = (lane > 0).astype(F32).astype(BF16)
    ones = jnp.where(
        ((row16 == 0) & (lane16 < W - 1)) | (row16 == 1) | ((row16 == 2) & (lane16 > 0)),
        1.0, 0.0,
    ).astype(BF16)
    for h in range(H):
        right_ref[192:208, h * W : (h + 1) * W] = ones
    acc_ref[...] = jnp.zeros(acc_ref.shape, F32)
    first = jnp.where(iota((16, HW), 0) == 0, 1.0, 0.0).astype(BF16)

    def gather(z, carry):
        for h in range(H):
            span = slice(h * W, (h + 1) * W)
            cells = gm_ref[z + 1, :, span]
            right_ref[0:64, span] = pltpu.roll(cells, W - 1, 1) * keep0
            right_ref[64:128, span] = cells
            right_ref[128:192, span] = pltpu.roll(cells, 1, 1) * keep2
        left = [
            xb_ref[z + a, :, b * W : b * W + HW] for a in range(3) for b in range(3)
        ]
        left += [hid_ref[z + 1].astype(BF16), gm_ref[z + 1, C : 2 * C, :], first]
        acc_ref[...] += dot(jnp.concatenate(left, axis=0), right_ref[...], ((1,), (1,)))
        return carry

    lax.fori_loop(0, D, gather, 0)

    def put(row, slab):
        send_ref[pl.ds(row, C, stride=ROWS), :] = slab

    lane = iota((C, W), 1)
    pad = jnp.zeros((C, 48), F32)
    tile1 = [
        jnp.concatenate([acc_ref[C * i : C * (i + 1), 128:208], pad], axis=1)
        for i in range(10)
    ]
    for ab in range(9):
        put(ab, acc_ref[C * ab : C * (ab + 1), 0:128])
    for i in range(4):
        put(9 + i, jnp.where(lane < 64, tile1[i], pltpu.roll(tile1[4 + i], 64, 1)))
    put(13, jnp.where(lane < 64, tile1[8], acc_ref[288:320, 0:128]))
    counts = jnp.broadcast_to(pltpu.roll(acc_ref[352:353, 0:128], 64, 1), (C, W))
    counts = jnp.where(lane < 64, counts, 0.0)
    for ab in range(9):
        own = jnp.where((lane >= 64) & (lane < 67), tile1[ab], 0.0)
        counts = counts + pltpu.roll(own, 3 * ab, 1)
    counts = counts + pltpu.roll(jnp.where(lane == 65, tile1[9], 0.0), 26, 1)
    put(14, counts)
    put(15, jnp.zeros((C, W), F32))
    row = iota((C, W), 0)
    stats = pltpu.roll(acc_ref[320:352, 0:128], 64, 1)
    second = pltpu.roll(stats, 96, 1)
    swapped = jnp.where(lane < 16, pltpu.roll(stats, 112, 1), pltpu.roll(stats, 16, 1))
    mine = (row < 16) == (lane < 16)
    table = jnp.where(lane < C, jnp.where(mine, second, swapped), 0.0)
    packed = table[0:8]
    for q in range(1, 4):
        packed = packed + pltpu.roll(table[8 * q : 8 * q + 8], 32 * q, 1)
    for r in range(8):
        put(16 + r, jnp.broadcast_to(packed[r : r + 1], (C, W)))


def whiten_terms(stats, count):
    gf_row = stats[14:15, 0:C]
    first_row = stats[14:15, C : 2 * C]
    packed = stats[16:24]
    table = jnp.concatenate([pltpu.roll(packed, (W - 32 * q) % W, 1) for q in range(4)], axis=0)
    table = table[:, 0:C]
    row = iota((C, C), 0)
    col = iota((C, C), 1)
    mine = (row < 16) == (col < 16)
    eye = (row == col).astype(F32)
    low = iota((1, C), 1) < 16
    second = jnp.where(mine, table, 0.0)
    other = jnp.concatenate([table[:, 16:32], table[:, 0:16]], axis=1)
    grad_mat = jnp.where(mine, other, 0.0).T

    def column(values):
        return jnp.sum(eye * values, axis=1, keepdims=True)

    def per_group(values):
        left = jnp.sum(jnp.where(low, values, 0.0), axis=1, keepdims=True)
        right = jnp.sum(jnp.where(low, 0.0, values), axis=1, keepdims=True)
        return jnp.where(low, left, right)

    avg = first_row / count
    avg_col = column(avg)
    cov = second / count - jnp.where(mine, avg_col * avg, 0.0) + EPSILON * eye
    trace = per_group(jnp.sum(cov * eye, axis=0, keepdims=True))
    normed = cov / trace
    project = 1.5 * eye - 0.5 * normed
    saved = []
    for step in range(NEWTON - 1):
        both = dot_high(project, jnp.concatenate([project, normed], axis=1))
        square, pn = both[:, 0:C], both[:, C : 2 * C]
        three = dot_high(square, jnp.concatenate([pn, project, normed], axis=1))
        saved.append((
            jnp.concatenate([project, square, three[:, C : 2 * C]], axis=0),
            jnp.concatenate([three[:, 2 * C : 3 * C], pn, normed], axis=0),
        ))
        project = 1.5 * project - 0.5 * three[:, 0:C]
    root = jnp.sqrt(trace)
    whiten = project / root
    offset_col = jnp.sum(whiten * avg, axis=1, keepdims=True)

    d_whiten = grad_mat - jnp.where(mine, column(gf_row) * avg, 0.0)
    d_project = d_whiten / root
    d_normed = jnp.zeros((C, C), F32)
    for powers, tail in reversed(saved):
        delta = -0.5 * d_project
        ahead = dot_high(powers, delta)
        d_normed = d_normed + ahead[2 * C : 3 * C]
        terms = jnp.concatenate([delta, ahead[0:C], ahead[C : 2 * C]], axis=1)
        d_project = 1.5 * d_project + dot_high(terms, tail)
    d_normed = d_normed - 0.5 * d_project
    d_trace = jnp.sum(-0.5 * d_whiten * whiten - d_normed * normed, axis=0, keepdims=True)
    d_trace = per_group(d_trace) / trace
    d_cov = d_normed / trace + d_trace * eye
    both = d_cov + d_cov.T
    d_avg = -(dot_high(gf_row, whiten) + dot_high(avg, both))
    return whiten, offset_col, both / count, d_avg / count, column


def grads_kernel(count, place_ref, pay_ref, gm_ref, dk_ref, w_ref, white_ref, dvol_ref, row_ref,
                 dh_ref, taps_ref, out_ref):
    stats = jnp.sum(pay_ref[...], axis=0)
    whiten, offset_col, symmetric, d_first, column = whiten_terms(stats, count)
    weight = w_ref[...].astype(F32)
    from_g = dot_high(weight, whiten, ((0,), (1,)))
    from_m = dot_high(weight, symmetric, ((0,), (0,)))
    bias = dot_high(d_first, weight)
    bias_col = column(bias)
    hidden_mat = jnp.concatenate([from_g, from_m], axis=1)
    full = jnp.concatenate(
        [hidden_mat, jnp.concatenate([jnp.zeros((C, C), F32), whiten], axis=1)], axis=0
    )
    coarse = full.astype(BF16)
    fine = (full - coarse.astype(F32)).astype(BF16)
    left = jnp.concatenate([coarse, fine], axis=1)

    mine = place_ref[0]
    pick = (iota((C, 1), 0) == mine).astype(F32)
    chosen = jnp.sum(pick * hidden_mat, axis=0, keepdims=True)
    chosen_bias = jnp.sum(pick * bias_col, axis=0, keepdims=True)
    prod = stats[0:16] * jnp.concatenate([chosen, chosen], axis=1)
    lane16 = iota((16, W), 1)
    row16 = iota((16, W), 0)
    low = jnp.sum(jnp.where(lane16 < 64, prod, 0.0), axis=1, keepdims=True)
    high = jnp.sum(jnp.where(lane16 < 64, 0.0, prod), axis=1, keepdims=True)
    to_low = jnp.where(row16 < 9, C + 3 * row16, C + 3 * (row16 - 9) + 2)
    to_low = jnp.where(row16 == 13, C + 26, jnp.where(row16 > 13, -1, to_low))
    to_high = jnp.where(row16 < 9, C + 3 * row16 + 1, C + 3 * (row16 - 5) + 2)
    to_high = jnp.where(row16 > 12, -1, to_high)
    taps_row = jnp.where(lane16 == to_low, low, 0.0) + jnp.where(lane16 == to_high, high, 0.0)
    taps_row = jnp.sum(taps_row, axis=0, keepdims=True)
    lane = iota((1, W), 1)
    ones_row = jnp.where((lane >= 64) & (lane < 91), stats[14:15], 0.0)
    taps_row = taps_row + chosen_bias * pltpu.roll(ones_row, W - 32, 1)
    hidden_sum = jnp.sum(jnp.where(lane == 91, stats[14:15], 0.0), axis=1, keepdims=True)
    pair = pltpu.roll(stats[13:14], 64, 1)[:, 0:64]
    point = dot_high(pair, jnp.concatenate([whiten, symmetric], axis=0)) + hidden_sum * d_first
    point = jnp.concatenate([point, jnp.zeros((1, W - C), F32)], axis=1)
    row = (taps_row + point) * (1.0 / math.sqrt(count))
    row_ref[...] = jnp.broadcast_to(row, (C, W))

    zeros = jnp.zeros((D + 2, C, W), F32)
    dh_ref[:, :, 0:W] = zeros
    dh_ref[:, :, PW - W : PW] = zeros
    inside_lo = place_ref[1].astype(F32)
    inside_hi = place_ref[2].astype(F32)

    for p in range(D + 2):
        cells = gm_ref[p]
        both = dot(left, jnp.concatenate([cells, cells], axis=0))
        d_hidden = both[0:C] + bias_col
        if p == 0:
            d_hidden = d_hidden * inside_lo
        elif p > D:
            d_hidden = d_hidden * inside_hi
        else:
            white = (both[C : 2 * C] - offset_col).astype(BF16)
            white_ref[:, p - 1] = white.reshape(C, H, W)
        dh_ref[p, :, W : W + HW] = d_hidden
    spread_taps(dk_ref, taps_ref, True)
    stencil(dh_ref, taps_ref, out_ref, D)
    for z in range(D):
        dvol_ref[:, z] = out_ref[z].astype(BF16).reshape(C, H, W)


def on_device(volumes, depth_kernel, point_weight, cotangent):
    x = volumes[0]
    g = cotangent[0]
    samples = lax.axis_size("sample")
    slabs = lax.axis_size("space")
    count = float(D * HW * samples * slabs)
    forward = [(i, i + 1) for i in range(slabs - 1)]
    backward = [(i + 1, i) for i in range(slabs - 1)]
    lo = lax.ppermute(jnp.concatenate([x[:, D - 2 :], g[:, D - 1 :]], axis=1), "space", forward)
    hi = lax.ppermute(jnp.concatenate([x[:, :2], g[:, :1]], axis=1), "space", backward)
    gm, send = pl.pallas_call(
        sums_kernel,
        out_shape=(
            jax.ShapeDtypeStruct((D + 2, 2 * C, HW), BF16),
            jax.ShapeDtypeStruct((C * ROWS, W), F32),
        ),
        scratch_shapes=[
            pltpu.VMEM((D + 4, C, PW), F32),
            pltpu.VMEM((D + 2, C, PW), BF16),
            pltpu.VMEM((D + 2, C, HW), F32),
            pltpu.VMEM((27, C, W), F32),
            pltpu.VMEM((208, HW), BF16),
            pltpu.VMEM((368, 208), F32),
        ],
        name="sums",
    )(x, g, lo, hi, depth_kernel, point_weight)
    parts = lax.all_to_all(send.reshape(C, ROWS, W), "sample", 0, 0)
    part = jnp.sum(parts, axis=0)
    pay = lax.all_to_all(jnp.broadcast_to(part, (slabs, ROWS, W)), "space", 0, 0)
    slab = lax.axis_index("space")
    place = jnp.stack([
        lax.axis_index("sample"),
        (slab > 0).astype(jnp.int32),
        (slab < slabs - 1).astype(jnp.int32),
    ])
    vmem = pl.BlockSpec(memory_space=pltpu.VMEM)
    white, d_volume, row = pl.pallas_call(
        lambda *refs: grads_kernel(count, *refs),
        in_specs=[pl.BlockSpec(memory_space=pltpu.SMEM)] + [vmem] * 4,
        out_shape=(
            jax.ShapeDtypeStruct((C, D, H, W), BF16),
            jax.ShapeDtypeStruct((C, D, H, W), BF16),
            jax.ShapeDtypeStruct((C, W), F32),
        ),
        scratch_shapes=[
            pltpu.VMEM((D + 2, C, PW), F32),
            pltpu.VMEM((27, C, W), F32),
            pltpu.VMEM((D, C, HW), F32),
        ],
        name="grads",
    )(place, pay, gm, depth_kernel, point_weight)
    rows = lax.all_to_all(row.reshape(C, 1, W), "sample", 0, 0).reshape(C, W)
    return white[None], d_volume[None], rows[:, 0:C].T, rows[:, C : C + 27]


def solution(mesh):
    split = P("sample", None, "space", None, None)
    return jax.shard_map(
        on_device,
        mesh=mesh,
        in_specs=(split, P(), P(), split),
        out_specs=(split, split, P(), P()),
        check_vma=False,
    )
```

```python
import math

import jax
import jax.numpy as jnp
from jax import lax
from jax.experimental import pallas as pl
from jax.experimental.pallas import tpu as pltpu
from jax.sharding import PartitionSpec as P


NEWTON = 5
EPSILON = 1e-05
C = 32
D = 4
H = 16
W = 128
HW = H * W
PW = (H + 2) * W
ROWS = 24
HIGH = lax.Precision.HIGHEST
F32 = jnp.float32
BF16 = jnp.bfloat16


def dot(a, b, dims=((1,), (0,)), precision=None):
    return lax.dot_general(
        a, b, (dims, ((), ())), precision=precision, preferred_element_type=F32
    )


def dot_high(a, b, dims=((1,), (0,))):
    return dot(a, b, dims, HIGH)


def iota(shape, dim):
    return lax.broadcasted_iota(jnp.int32, shape, dim)


def spread_taps(dk_ref, taps_ref, flip):
    for t in range(27):
        s = 26 - t if flip else t
        taps_ref[t] = jnp.broadcast_to(dk_ref[:, s : s + 1], (C, W))


def stencil(src_ref, taps_ref, dst_ref, planes, step=1):
    lane = iota((8, W), 1)
    for group in range(C // 8):
        rows = pl.ds(8 * group, 8)
        taps = [taps_ref[t, rows, :] for t in range(27)]

        def plane(p, carry):
            for h in range(H):
                parts = [None, None, None]
                for a in range(3):
                    for b in range(3):
                        cells = src_ref[step * p + a, rows, (h + b) * W : (h + b + 1) * W]
                        for e in range(3):
                            term = taps[9 * a + 3 * b + e] * cells
                            parts[e] = term if parts[e] is None else parts[e] + term
                left = jnp.where(lane == 0, 0.0, pltpu.roll(parts[0], 1, 1))
                right = jnp.where(lane == W - 1, 0.0, pltpu.roll(parts[2], W - 1, 1))
                dst_ref[p, rows, h * W : (h + 1) * W] = parts[1] + left + right
            return carry

        lax.fori_loop(0, planes, plane, 0)


def slab_sums(xs, gs, step, dk_ref, w_ref, gm_refs, acc_ref,
              xf_ref, xb_ref, hid_ref, taps_ref, right_ref):
    zeros = jnp.zeros((len(xs), C, W), F32)
    xf_ref[:, :, 0:W] = zeros
    xf_ref[:, :, PW - W : PW] = zeros
    xb_ref[:, :, 0:W] = zeros.astype(BF16)
    xb_ref[:, :, PW - W : PW] = zeros.astype(BF16)
    for p, cells in enumerate(xs):
        cells = cells().reshape(C, HW)
        xf_ref[p, :, W : W + HW] = cells.astype(F32)
        xb_ref[p, :, W : W + HW] = cells
    spread_taps(dk_ref, taps_ref, False)
    stencil(xf_ref, taps_ref, hid_ref, 2, step)

    lane = iota((1, W), 1)
    row16 = iota((16, W), 0)
    lane16 = iota((16, W), 1)
    keep0 = (lane < W - 1).astype(F32).astype(BF16)
    keep2 = (lane > 0).astype(F32).astype(BF16)
    ones = jnp.where(
        ((row16 == 0) & (lane16 < W - 1)) | (row16 == 1) | ((row16 == 2) & (lane16 > 0)),
        1.0, 0.0,
    ).astype(BF16)
    for h in range(H):
        right_ref[192:208, h * W : (h + 1) * W] = ones
    first = jnp.where(iota((16, HW), 0) == 0, 1.0, 0.0).astype(BF16)
    for i in range(2):
        hidden = hid_ref[i].astype(BF16)
        mixed = dot(w_ref[...], hidden).astype(BF16)
        gm_refs[i][0:C, :] = gs[i]().reshape(C, HW)
        gm_refs[i][C : 2 * C, :] = mixed
        for h in range(H):
            span = slice(h * W, (h + 1) * W)
            cells = gm_refs[i][:, span]
            right_ref[0:64, span] = pltpu.roll(cells, W - 1, 1) * keep0
            right_ref[64:128, span] = cells
            right_ref[128:192, span] = pltpu.roll(cells, 1, 1) * keep2
        left = [
            xb_ref[step * i + a, :, b * W : b * W + HW] for a in range(3) for b in range(3)
        ]
        left += [hidden, mixed, first]
        acc_ref[:, 0:208] += dot(
            jnp.concatenate(left, axis=0), right_ref[...], ((1,), (1,))
        )


def inner_kernel(x_ref, g_ref, dk_ref, w_ref, gm_ref, acc_ref, *scratch):
    acc_ref[...] = jnp.zeros(acc_ref.shape, F32)
    xs = [lambda p=p: x_ref[:, p] for p in range(D)]
    gs = [lambda p=p: g_ref[:, p] for p in (1, 2)]
    slab_sums(xs, gs, 1, dk_ref, w_ref, (gm_ref.at[0], gm_ref.at[1]), acc_ref, *scratch)


def outer_kernel(x_ref, g_ref, lo_ref, hi_ref, dk_ref, w_ref, part_ref,
                 gm_lo_ref, gm_hi_ref, send_ref, acc_ref, *scratch):
    acc_ref[...] = part_ref[...]
    xs = [lambda: lo_ref[:, 0]] + [lambda p=p: x_ref[:, p] for p in range(D)]
    xs += [lambda: hi_ref[:, 0]]
    gs = [lambda p=p: g_ref[:, p] for p in (0, 3)]
    slab_sums(xs, gs, 3, dk_ref, w_ref, (gm_lo_ref, gm_hi_ref), acc_ref, *scratch)

    def put(row, slab):
        send_ref[pl.ds(row, C, stride=ROWS), :] = slab

    lane = iota((C, W), 1)
    tile1 = [acc_ref[C * i : C * (i + 1), 128:256] for i in range(10)]
    for ab in range(9):
        put(ab, acc_ref[C * ab : C * (ab + 1), 0:128])
    for i in range(4):
        put(9 + i, jnp.where(lane < 64, tile1[i], pltpu.roll(tile1[4 + i], 64, 1)))
    put(13, jnp.where(lane < 64, tile1[8], acc_ref[288:320, 0:128]))
    counts = jnp.broadcast_to(pltpu.roll(acc_ref[352:353, 0:128], 64, 1), (C, W))
    counts = jnp.where(lane < 64, counts, 0.0)
    for ab in range(9):
        own = jnp.where((lane >= 64) & (lane < 67), tile1[ab], 0.0)
        counts = counts + pltpu.roll(own, 3 * ab, 1)
    counts = counts + pltpu.roll(jnp.where(lane == 65, tile1[9], 0.0), 26, 1)
    put(14, counts)
    put(15, jnp.zeros((C, W), F32))
    row = iota((C, W), 0)
    stats = pltpu.roll(acc_ref[320:352, 0:128], 64, 1)
    second = pltpu.roll(stats, 96, 1)
    swapped = jnp.where(lane < 16, pltpu.roll(stats, 112, 1), pltpu.roll(stats, 16, 1))
    mine = (row < 16) == (lane < 16)
    table = jnp.where(lane < C, jnp.where(mine, second, swapped), 0.0)
    packed = table[0:8]
    for q in range(1, 4):
        packed = packed + pltpu.roll(table[8 * q : 8 * q + 8], 32 * q, 1)
    for r in range(8):
        put(16 + r, jnp.broadcast_to(packed[r : r + 1], (C, W)))


def whiten_terms(stats, count):
    gf_row = stats[14:15, 0:C]
    first_row = stats[14:15, C : 2 * C]
    packed = stats[16:24]
    table = jnp.concatenate([pltpu.roll(packed, (W - 32 * q) % W, 1) for q in range(4)], axis=0)
    table = table[:, 0:C]
    row = iota((C, C), 0)
    col = iota((C, C), 1)
    mine = (row < 16) == (col < 16)
    eye = (row == col).astype(F32)
    low = iota((1, C), 1) < 16
    second = jnp.where(mine, table, 0.0)
    other = jnp.concatenate([table[:, 16:32], table[:, 0:16]], axis=1)
    grad_mat = jnp.where(mine, other, 0.0).T

    def column(values):
        return jnp.sum(eye * values, axis=1, keepdims=True)

    def per_group(values):
        left = jnp.sum(jnp.where(low, values, 0.0), axis=1, keepdims=True)
        right = jnp.sum(jnp.where(low, 0.0, values), axis=1, keepdims=True)
        return jnp.where(low, left, right)

    avg = first_row / count
    avg_col = column(avg)
    cov = second / count - jnp.where(mine, avg_col * avg, 0.0) + EPSILON * eye
    trace = per_group(jnp.sum(cov * eye, axis=0, keepdims=True))
    normed = cov / trace
    project = 1.5 * eye - 0.5 * normed
    saved = []
    for _ in range(NEWTON - 1):
        both = dot_high(project, jnp.concatenate([project, normed], axis=1))
        square, pn = both[:, 0:C], both[:, C : 2 * C]
        three = dot_high(square, jnp.concatenate([pn, project, normed], axis=1))
        saved.append((
            jnp.concatenate([project, square, three[:, C : 2 * C]], axis=0),
            jnp.concatenate([three[:, 2 * C : 3 * C], pn, normed], axis=0),
        ))
        project = 1.5 * project - 0.5 * three[:, 0:C]
    root = jnp.sqrt(trace)
    whiten = project / root
    offset_col = jnp.sum(whiten * avg, axis=1, keepdims=True)

    d_whiten = grad_mat - jnp.where(mine, column(gf_row) * avg, 0.0)
    d_project = d_whiten / root
    d_normed = jnp.zeros((C, C), F32)
    for powers, tail in reversed(saved):
        delta = -0.5 * d_project
        ahead = dot_high(powers, delta)
        d_normed = d_normed + ahead[2 * C : 3 * C]
        terms = jnp.concatenate([delta, ahead[0:C], ahead[C : 2 * C]], axis=1)
        d_project = 1.5 * d_project + dot_high(terms, tail)
    d_normed = d_normed - 0.5 * d_project
    d_trace = jnp.sum(-0.5 * d_whiten * whiten - d_normed * normed, axis=0, keepdims=True)
    d_trace = per_group(d_trace) / trace
    d_cov = d_normed / trace + d_trace * eye
    both = d_cov + d_cov.T
    d_avg = -(dot_high(gf_row, whiten) + dot_high(avg, both))
    return whiten, offset_col, both / count, d_avg / count, column


def terms_kernel(count, place_ref, pay_ref, w_ref, left_ref, shift_ref, row_ref):
    stats = jnp.sum(pay_ref[...], axis=0)
    whiten, offset_col, symmetric, d_first, column = whiten_terms(stats, count)
    weight = w_ref[...].astype(F32)
    from_g = dot_high(weight, whiten, ((0,), (1,)))
    from_m = dot_high(weight, symmetric, ((0,), (0,)))
    bias_col = column(dot_high(d_first, weight))
    hidden_mat = jnp.concatenate([from_g, from_m], axis=1)
    full = jnp.concatenate(
        [hidden_mat, jnp.concatenate([jnp.zeros((C, C), F32), whiten], axis=1)], axis=0
    )
    coarse = full.astype(BF16)
    fine = (full - coarse.astype(F32)).astype(BF16)
    left_ref[...] = jnp.concatenate([coarse, fine], axis=1)
    shift_ref[0:C] = jnp.broadcast_to(bias_col, (C, W))
    shift_ref[C : 2 * C] = jnp.broadcast_to(-offset_col, (C, W))

    mine = place_ref[0]
    pick = (iota((C, 1), 0) == mine).astype(F32)
    chosen = jnp.sum(pick * hidden_mat, axis=0, keepdims=True)
    chosen_bias = jnp.sum(pick * bias_col, axis=0, keepdims=True)
    prod = stats[0:16] * jnp.concatenate([chosen, chosen], axis=1)
    lane16 = iota((16, W), 1)
    row16 = iota((16, W), 0)
    low = jnp.sum(jnp.where(lane16 < 64, prod, 0.0), axis=1, keepdims=True)
    high = jnp.sum(jnp.where(lane16 < 64, 0.0, prod), axis=1, keepdims=True)
    to_low = jnp.where(row16 < 9, C + 3 * row16, C + 3 * (row16 - 9) + 2)
    to_low = jnp.where(row16 == 13, C + 26, jnp.where(row16 > 13, -1, to_low))
    to_high = jnp.where(row16 < 9, C + 3 * row16 + 1, C + 3 * (row16 - 5) + 2)
    to_high = jnp.where(row16 > 12, -1, to_high)
    taps_row = jnp.where(lane16 == to_low, low, 0.0) + jnp.where(lane16 == to_high, high, 0.0)
    taps_row = jnp.sum(taps_row, axis=0, keepdims=True)
    lane = iota((1, W), 1)
    ones_row = jnp.where((lane >= 64) & (lane < 91), stats[14:15], 0.0)
    taps_row = taps_row + chosen_bias * pltpu.roll(ones_row, W - 32, 1)
    hidden_sum = jnp.sum(jnp.where(lane == 91, stats[14:15], 0.0), axis=1, keepdims=True)
    pair = pltpu.roll(stats[13:14], 64, 1)[:, 0:64]
    point = dot_high(pair, jnp.concatenate([whiten, symmetric], axis=0)) + hidden_sum * d_first
    point = jnp.concatenate([point, jnp.zeros((1, W - C), F32)], axis=1)
    row = (taps_row + point) * (1.0 / math.sqrt(count))
    row_ref[...] = jnp.broadcast_to(row, (C, W))


def grads_kernel(place_ref, left_ref, shift_ref, lo_ref, first_ref, inner_ref, last_ref, hi_ref,
                 dk_ref, white_ref, dvol_ref, dh_ref, taps_ref, out_ref):
    zeros = jnp.zeros((D + 2, C, W), F32)
    dh_ref[:, :, 0:W] = zeros
    dh_ref[:, :, PW - W : PW] = zeros
    inside_lo = place_ref[1].astype(F32)
    inside_hi = place_ref[2].astype(F32)
    left = left_ref[...]
    bias = shift_ref[0:C, 0:1]
    minus_offset = shift_ref[C : 2 * C, 0:1]
    planes = [lo_ref, first_ref, inner_ref.at[0], inner_ref.at[1], last_ref, hi_ref]
    for p in range(D + 2):
        cells = planes[p][...]
        both = dot(left, jnp.concatenate([cells, cells], axis=0))
        d_hidden = both[0:C] + bias
        if p == 0:
            d_hidden = d_hidden * inside_lo
        elif p > D:
            d_hidden = d_hidden * inside_hi
        else:
            white = (both[C : 2 * C] + minus_offset).astype(BF16)
            white_ref[:, p - 1] = white.reshape(C, H, W)
        dh_ref[p, :, W : W + HW] = d_hidden
    spread_taps(dk_ref, taps_ref, True)
    stencil(dh_ref, taps_ref, out_ref, D)
    for z in range(D):
        dvol_ref[:, z] = out_ref[z].astype(BF16).reshape(C, H, W)


def cost(us):
    return pl.CostEstimate(flops=int(us * 1e8), bytes_accessed=int(us * 1e6), transcendentals=0)


def whole_step(volumes, depth_kernel, point_weight, cotangent):
    x = volumes[0]
    g = cotangent[0]
    samples = lax.axis_size("sample")
    slabs = lax.axis_size("space")
    count = float(D * HW * samples * slabs)
    forward = [(i, i + 1) for i in range(slabs - 1)]
    backward = [(i + 1, i) for i in range(slabs - 1)]
    scratch = lambda planes: [
        pltpu.VMEM((planes, C, PW), F32),
        pltpu.VMEM((planes, C, PW), BF16),
        pltpu.VMEM((2, C, HW), F32),
        pltpu.VMEM((27, C, W), F32),
        pltpu.VMEM((208, HW), BF16),
    ]
    vmem = pl.BlockSpec(memory_space=pltpu.VMEM)
    smem = pl.BlockSpec(memory_space=pltpu.SMEM)
    shape = jax.ShapeDtypeStruct

    x_lo = lax.ppermute(x[:, D - 1 :], "space", forward)
    x_hi = lax.ppermute(x[:, :1], "space", backward)
    gm_inner, acc = pl.pallas_call(
        inner_kernel,
        out_shape=(shape((2, 2 * C, HW), BF16), shape((368, 256), F32)),
        scratch_shapes=scratch(D),
        cost_estimate=cost(6),
        name="inner",
    )(x, g, depth_kernel, point_weight)
    gm_first, gm_last, send = pl.pallas_call(
        outer_kernel,
        out_shape=(
            shape((2 * C, HW), BF16),
            shape((2 * C, HW), BF16),
            shape((C * ROWS, W), F32),
        ),
        scratch_shapes=[pltpu.VMEM((368, 256), F32)] + scratch(D + 2),
        cost_estimate=cost(6),
        name="outer",
    )(x, g, x_lo, x_hi, depth_kernel, point_weight, acc)
    gm_lo = lax.ppermute(gm_last, "space", forward)
    gm_hi = lax.ppermute(gm_first, "space", backward)
    parts = lax.all_to_all(send.reshape(C, ROWS, W), "sample", 0, 0)
    part = jnp.sum(parts, axis=0)
    pay = lax.all_to_all(jnp.broadcast_to(part, (slabs, ROWS, W)), "space", 0, 0)
    slab = lax.axis_index("space")
    place = jnp.stack([
        lax.axis_index("sample"),
        (slab > 0).astype(jnp.int32),
        (slab < slabs - 1).astype(jnp.int32),
    ])
    left, shift, row = pl.pallas_call(
        lambda *refs: terms_kernel(count, *refs),
        in_specs=[smem] + [vmem] * 2,
        out_shape=(shape((2 * C, 4 * C), BF16), shape((2 * C, W), F32), shape((C, W), F32)),
        cost_estimate=cost(4),
        name="terms",
    )(place, pay, point_weight)
    rows = lax.all_to_all(row.reshape(C, 1, W), "sample", 0, 0).reshape(C, W)
    white, d_volume = pl.pallas_call(
        grads_kernel,
        in_specs=[smem] + [vmem] * 8,
        out_shape=(shape((C, D, H, W), BF16), shape((C, D, H, W), BF16)),
        scratch_shapes=[
            pltpu.VMEM((D + 2, C, PW), F32),
            pltpu.VMEM((27, C, W), F32),
            pltpu.VMEM((D, C, HW), F32),
        ],
        cost_estimate=cost(8),
        name="grads",
    )(place, left, shift, gm_lo, gm_first, gm_inner, gm_last, gm_hi, depth_kernel)
    return white[None], d_volume[None], rows[:, 0:C].T, rows[:, C : C + 27]


def solution(mesh):
    split = P("sample", None, "space", None, None)
    return jax.shard_map(
        whole_step,
        mesh=mesh,
        in_specs=(split, P(), P(), split),
        out_specs=(split, split, P(), P()),
        check_vma=False,
    )
```

```python
import math

import jax
import jax.numpy as jnp
from jax import lax
from jax.experimental import pallas as pl
from jax.experimental.pallas import tpu as pltpu
from jax.sharding import PartitionSpec as P

NEWTON = 5
EPSILON = 1e-05
C = 32
D = 4
H = 16
W = 128
HW = H * W
PW = (H + 2) * W
ROWS = 24
HIGH = lax.Precision.HIGHEST
F32 = jnp.float32
BF16 = jnp.bfloat16


def dot(a, b, dims=((1,), (0,)), precision=None):
    return lax.dot_general(
        a, b, (dims, ((), ())), precision=precision, preferred_element_type=F32
    )


def dot_high(a, b, dims=((1,), (0,))):
    return dot(a, b, dims, HIGH)


def iota(shape, dim):
    return lax.broadcasted_iota(jnp.int32, shape, dim)


def spread_taps(dk_ref, taps_ref, flip):
    for t in range(27):
        s = 26 - t if flip else t
        taps_ref[t] = jnp.broadcast_to(dk_ref[:, s : s + 1], (C, W))


def stencil(src_ref, taps_ref, dst_ref, planes, step=1):
    lane = iota((8, W), 1)
    for group in range(C // 8):
        rows = pl.ds(8 * group, 8)
        taps = [taps_ref[t, rows, :] for t in range(27)]

        def plane(p, carry):
            for h in range(H):
                parts = [None, None, None]
                for a in range(3):
                    for b in range(3):
                        cells = src_ref[step * p + a, rows, (h + b) * W : (h + b + 1) * W]
                        for e in range(3):
                            term = taps[9 * a + 3 * b + e] * cells
                            parts[e] = term if parts[e] is None else parts[e] + term
                left = jnp.where(lane == 0, 0.0, pltpu.roll(parts[0], 1, 1))
                right = jnp.where(lane == W - 1, 0.0, pltpu.roll(parts[2], W - 1, 1))
                dst_ref[p, rows, h * W : (h + 1) * W] = parts[1] + left + right
            return carry

        lax.fori_loop(0, planes, plane, 0)


def slab_sums(xs, gs, step, dk_ref, w_ref, gm_refs, acc_ref,
              xf_ref, xb_ref, hid_ref, taps_ref, right_ref):
    zeros = jnp.zeros((len(xs), C, W), F32)
    xf_ref[:, :, 0:W] = zeros
    xf_ref[:, :, PW - W : PW] = zeros
    xb_ref[:, :, 0:W] = zeros.astype(BF16)
    xb_ref[:, :, PW - W : PW] = zeros.astype(BF16)
    for p, cells in enumerate(xs):
        cells = cells().reshape(C, HW)
        xf_ref[p, :, W : W + HW] = cells.astype(F32)
        xb_ref[p, :, W : W + HW] = cells
    spread_taps(dk_ref, taps_ref, False)
    stencil(xf_ref, taps_ref, hid_ref, 2, step)

    lane = iota((1, W), 1)
    row16 = iota((16, W), 0)
    lane16 = iota((16, W), 1)
    keep0 = (lane < W - 1).astype(F32).astype(BF16)
    keep2 = (lane > 0).astype(F32).astype(BF16)
    ones = jnp.where(
        ((row16 == 0) & (lane16 < W - 1)) | (row16 == 1) | ((row16 == 2) & (lane16 > 0)),
        1.0, 0.0,
    ).astype(BF16)
    for h in range(H):
        right_ref[192:208, h * W : (h + 1) * W] = ones
    first = jnp.where(iota((16, HW), 0) == 0, 1.0, 0.0).astype(BF16)
    for i in range(2):
        hidden = hid_ref[i].astype(BF16)
        mixed = dot(w_ref[...], hidden).astype(BF16)
        gm_refs[i][0:C, :] = gs[i]().reshape(C, HW)
        gm_refs[i][C : 2 * C, :] = mixed
        for h in range(H):
            span = slice(h * W, (h + 1) * W)
            cells = gm_refs[i][:, span]
            right_ref[0:64, span] = pltpu.roll(cells, W - 1, 1) * keep0
            right_ref[64:128, span] = cells
            right_ref[128:192, span] = pltpu.roll(cells, 1, 1) * keep2
        left = [
            xb_ref[step * i + a, :, b * W : b * W + HW] for a in range(3) for b in range(3)
        ]
        left += [hidden, mixed, first]
        acc_ref[:, 0:208] += dot(
            jnp.concatenate(left, axis=0), right_ref[...], ((1,), (1,))
        )


def edges_kernel(x_ref, first_ref, last_ref, sems):
    first = pltpu.make_async_copy(x_ref.at[:, 0], first_ref, sems.at[0])
    last = pltpu.make_async_copy(x_ref.at[:, D - 1], last_ref, sems.at[1])
    first.start()
    last.start()
    first.wait()
    last.wait()


def inner_kernel(x_ref, g_ref, dk_ref, w_ref, gm_ref, acc_ref, *scratch):
    acc_ref[...] = jnp.zeros(acc_ref.shape, F32)
    xs = [lambda p=p: x_ref[:, p] for p in range(D)]
    gs = [lambda p=p: g_ref[:, p] for p in (1, 2)]
    slab_sums(xs, gs, 1, dk_ref, w_ref, (gm_ref.at[0], gm_ref.at[1]), acc_ref, *scratch)


def outer_kernel(x_ref, g_ref, lo_ref, hi_ref, dk_ref, w_ref, part_ref,
                 gm_lo_ref, gm_hi_ref, send_ref, acc_ref, *scratch):
    acc_ref[...] = part_ref[...]
    xs = [lambda: lo_ref[...]] + [lambda p=p: x_ref[:, p] for p in range(D)]
    xs += [lambda: hi_ref[...]]
    gs = [lambda p=p: g_ref[:, p] for p in (0, 3)]
    slab_sums(xs, gs, 3, dk_ref, w_ref, (gm_lo_ref, gm_hi_ref), acc_ref, *scratch)

    def put(row, slab):
        send_ref[pl.ds(row, C, stride=ROWS), :] = slab

    lane = iota((C, W), 1)
    tile1 = [acc_ref[C * i : C * (i + 1), 128:256] for i in range(10)]
    for ab in range(9):
        put(ab, acc_ref[C * ab : C * (ab + 1), 0:128])
    for i in range(4):
        put(9 + i, jnp.where(lane < 64, tile1[i], pltpu.roll(tile1[4 + i], 64, 1)))
    put(13, jnp.where(lane < 64, tile1[8], acc_ref[288:320, 0:128]))
    counts = jnp.broadcast_to(pltpu.roll(acc_ref[352:353, 0:128], 64, 1), (C, W))
    counts = jnp.where(lane < 64, counts, 0.0)
    for ab in range(9):
        own = jnp.where((lane >= 64) & (lane < 67), tile1[ab], 0.0)
        counts = counts + pltpu.roll(own, 3 * ab, 1)
    counts = counts + pltpu.roll(jnp.where(lane == 65, tile1[9], 0.0), 26, 1)
    put(14, counts)
    put(15, jnp.zeros((C, W), F32))
    row = iota((C, W), 0)
    stats = pltpu.roll(acc_ref[320:352, 0:128], 64, 1)
    second = pltpu.roll(stats, 96, 1)
    swapped = jnp.where(lane < 16, pltpu.roll(stats, 112, 1), pltpu.roll(stats, 16, 1))
    mine = (row < 16) == (lane < 16)
    table = jnp.where(lane < C, jnp.where(mine, second, swapped), 0.0)
    packed = table[0:8]
    for q in range(1, 4):
        packed = packed + pltpu.roll(table[8 * q : 8 * q + 8], 32 * q, 1)
    for r in range(8):
        put(16 + r, jnp.broadcast_to(packed[r : r + 1], (C, W)))


def whiten_terms(stats, count):
    gf_row = stats[14:15, 0:C]
    first_row = stats[14:15, C : 2 * C]
    packed = stats[16:24]
    table = jnp.concatenate([pltpu.roll(packed, (W - 32 * q) % W, 1) for q in range(4)], axis=0)
    table = table[:, 0:C]
    row = iota((C, C), 0)
    col = iota((C, C), 1)
    mine = (row < 16) == (col < 16)
    eye = (row == col).astype(F32)
    low = iota((1, C), 1) < 16
    second = jnp.where(mine, table, 0.0)
    other = jnp.concatenate([table[:, 16:32], table[:, 0:16]], axis=1)
    grad_mat = jnp.where(mine, other, 0.0).T

    def column(values):
        return jnp.sum(eye * values, axis=1, keepdims=True)

    def per_group(values):
        left = jnp.sum(jnp.where(low, values, 0.0), axis=1, keepdims=True)
        right = jnp.sum(jnp.where(low, 0.0, values), axis=1, keepdims=True)
        return jnp.where(low, left, right)

    avg = first_row / count
    avg_col = column(avg)
    cov = second / count - jnp.where(mine, avg_col * avg, 0.0) + EPSILON * eye
    trace = per_group(jnp.sum(cov * eye, axis=0, keepdims=True))
    normed = cov / trace
    project = 1.5 * eye - 0.5 * normed
    saved = []
    for _ in range(NEWTON - 1):
        both = dot_high(project, jnp.concatenate([project, normed], axis=1))
        square, pn = both[:, 0:C], both[:, C : 2 * C]
        three = dot_high(square, jnp.concatenate([pn, project, normed], axis=1))
        saved.append((
            jnp.concatenate([project, square, three[:, C : 2 * C]], axis=0),
            jnp.concatenate([three[:, 2 * C : 3 * C], pn, normed], axis=0),
        ))
        project = 1.5 * project - 0.5 * three[:, 0:C]
    root = jnp.sqrt(trace)
    whiten = project / root
    offset_col = jnp.sum(whiten * avg, axis=1, keepdims=True)

    d_whiten = grad_mat - jnp.where(mine, column(gf_row) * avg, 0.0)
    d_project = d_whiten / root
    d_normed = jnp.zeros((C, C), F32)
    for powers, tail in reversed(saved):
        delta = -0.5 * d_project
        ahead = dot_high(powers, delta)
        d_normed = d_normed + ahead[2 * C : 3 * C]
        terms = jnp.concatenate([delta, ahead[0:C], ahead[C : 2 * C]], axis=1)
        d_project = 1.5 * d_project + dot_high(terms, tail)
    d_normed = d_normed - 0.5 * d_project
    d_trace = jnp.sum(-0.5 * d_whiten * whiten - d_normed * normed, axis=0, keepdims=True)
    d_trace = per_group(d_trace) / trace
    d_cov = d_normed / trace + d_trace * eye
    both = d_cov + d_cov.T
    d_avg = -(dot_high(gf_row, whiten) + dot_high(avg, both))
    return whiten, offset_col, both / count, d_avg / count, column


def terms_kernel(count, place_ref, pay_ref, w_ref, left_ref, shift_ref, row_ref):
    stats = jnp.sum(pay_ref[...], axis=0)
    whiten, offset_col, symmetric, d_first, column = whiten_terms(stats, count)
    weight = w_ref[...].astype(F32)
    from_g = dot_high(weight, whiten, ((0,), (1,)))
    from_m = dot_high(weight, symmetric, ((0,), (0,)))
    bias_col = column(dot_high(d_first, weight))
    hidden_mat = jnp.concatenate([from_g, from_m], axis=1)
    full = jnp.concatenate(
        [hidden_mat, jnp.concatenate([jnp.zeros((C, C), F32), whiten], axis=1)], axis=0
    )
    coarse = full.astype(BF16)
    fine = (full - coarse.astype(F32)).astype(BF16)
    left_ref[...] = jnp.concatenate([coarse, fine], axis=1)
    shift_ref[0:C] = jnp.broadcast_to(bias_col, (C, W))
    shift_ref[C : 2 * C] = jnp.broadcast_to(-offset_col, (C, W))

    mine = place_ref[0]
    pick = (iota((C, 1), 0) == mine).astype(F32)
    chosen = jnp.sum(pick * hidden_mat, axis=0, keepdims=True)
    chosen_bias = jnp.sum(pick * bias_col, axis=0, keepdims=True)
    prod = stats[0:16] * jnp.concatenate([chosen, chosen], axis=1)
    lane16 = iota((16, W), 1)
    row16 = iota((16, W), 0)
    low = jnp.sum(jnp.where(lane16 < 64, prod, 0.0), axis=1, keepdims=True)
    high = jnp.sum(jnp.where(lane16 < 64, 0.0, prod), axis=1, keepdims=True)
    to_low = jnp.where(row16 < 9, C + 3 * row16, C + 3 * (row16 - 9) + 2)
    to_low = jnp.where(row16 == 13, C + 26, jnp.where(row16 > 13, -1, to_low))
    to_high = jnp.where(row16 < 9, C + 3 * row16 + 1, C + 3 * (row16 - 5) + 2)
    to_high = jnp.where(row16 > 12, -1, to_high)
    taps_row = jnp.where(lane16 == to_low, low, 0.0) + jnp.where(lane16 == to_high, high, 0.0)
    taps_row = jnp.sum(taps_row, axis=0, keepdims=True)
    lane = iota((1, W), 1)
    ones_row = jnp.where((lane >= 64) & (lane < 91), stats[14:15], 0.0)
    taps_row = taps_row + chosen_bias * pltpu.roll(ones_row, W - 32, 1)
    hidden_sum = jnp.sum(jnp.where(lane == 91, stats[14:15], 0.0), axis=1, keepdims=True)
    pair = pltpu.roll(stats[13:14], 64, 1)[:, 0:64]
    point = dot_high(pair, jnp.concatenate([whiten, symmetric], axis=0)) + hidden_sum * d_first
    point = jnp.concatenate([point, jnp.zeros((1, W - C), F32)], axis=1)
    row = (taps_row + point) * (1.0 / math.sqrt(count))
    row_ref[...] = jnp.broadcast_to(row, (C, W))


def grads_kernel(place_ref, left_ref, shift_ref, lo_ref, first_ref, inner_ref, last_ref, hi_ref,
                 dk_ref, white_ref, dvol_ref, dh_ref, taps_ref, out_ref):
    zeros = jnp.zeros((D + 2, C, W), F32)
    dh_ref[:, :, 0:W] = zeros
    dh_ref[:, :, PW - W : PW] = zeros
    inside_lo = place_ref[1].astype(F32)
    inside_hi = place_ref[2].astype(F32)
    left = left_ref[...]
    bias = shift_ref[0:C, 0:1]
    minus_offset = shift_ref[C : 2 * C, 0:1]
    planes = [lo_ref, first_ref, inner_ref.at[0], inner_ref.at[1], last_ref, hi_ref]
    for p in range(D + 2):
        cells = planes[p][...]
        both = dot(left, jnp.concatenate([cells, cells], axis=0))
        d_hidden = both[0:C] + bias
        if p == 0:
            d_hidden = d_hidden * inside_lo
        elif p > D:
            d_hidden = d_hidden * inside_hi
        else:
            white = (both[C : 2 * C] + minus_offset).astype(BF16)
            white_ref[:, p - 1] = white.reshape(C, H, W)
        dh_ref[p, :, W : W + HW] = d_hidden
    spread_taps(dk_ref, taps_ref, True)
    stencil(dh_ref, taps_ref, out_ref, D)
    for z in range(D):
        dvol_ref[:, z] = out_ref[z].astype(BF16).reshape(C, H, W)


def cost(us):
    return pl.CostEstimate(flops=int(us * 1e8), bytes_accessed=int(us * 1e6), transcendentals=0)


def whole_step(volumes, depth_kernel, point_weight, cotangent):
    x = volumes[0]
    g = cotangent[0]
    samples = lax.axis_size("sample")
    slabs = lax.axis_size("space")
    count = float(D * HW * samples * slabs)
    forward = [(i, i + 1) for i in range(slabs - 1)]
    backward = [(i + 1, i) for i in range(slabs - 1)]
    scratch = lambda planes: [
        pltpu.VMEM((planes, C, PW), F32),
        pltpu.VMEM((planes, C, PW), BF16),
        pltpu.VMEM((2, C, HW), F32),
        pltpu.VMEM((27, C, W), F32),
        pltpu.VMEM((208, HW), BF16),
    ]
    vmem = pl.BlockSpec(memory_space=pltpu.VMEM)
    smem = pl.BlockSpec(memory_space=pltpu.SMEM)
    shape = jax.ShapeDtypeStruct
    near = lambda array: pltpu.with_memory_space_constraint(array, pltpu.VMEM)

    x_first, x_last = pl.pallas_call(
        edges_kernel,
        in_specs=[pl.BlockSpec(memory_space=pl.ANY)],
        out_shape=(pltpu.VMEM((C, H, W), BF16), pltpu.VMEM((C, H, W), BF16)),
        scratch_shapes=[pltpu.SemaphoreType.DMA((2,))],
        name="edges",
    )(x)
    x_lo = lax.ppermute(x_last, "space", forward)
    x_hi = lax.ppermute(x_first, "space", backward)
    gm_inner, acc = pl.pallas_call(
        inner_kernel,
        out_shape=(pltpu.VMEM((2, 2 * C, HW), BF16), pltpu.VMEM((368, 256), F32)),
        scratch_shapes=scratch(D),
        cost_estimate=cost(6),
        name="inner",
    )(x, g, depth_kernel, point_weight)
    gm_first, gm_last, send = pl.pallas_call(
        outer_kernel,
        out_shape=(
            pltpu.VMEM((2 * C, HW), BF16),
            pltpu.VMEM((2 * C, HW), BF16),
            pltpu.VMEM((C * ROWS, W), F32),
        ),
        scratch_shapes=[pltpu.VMEM((368, 256), F32)] + scratch(D + 2),
        cost_estimate=cost(6),
        name="outer",
    )(x, g, near(x_lo), near(x_hi), depth_kernel, point_weight, near(acc))
    gm_lo = lax.ppermute(gm_last, "space", forward)
    gm_hi = lax.ppermute(gm_first, "space", backward)
    parts = lax.all_to_all(send.reshape(C, ROWS, W), "sample", 0, 0)
    part = jnp.sum(parts, axis=0)
    pay = lax.all_to_all(jnp.broadcast_to(part, (slabs, ROWS, W)), "space", 0, 0)
    slab = lax.axis_index("space")
    place = jnp.stack([
        lax.axis_index("sample"),
        (slab > 0).astype(jnp.int32),
        (slab < slabs - 1).astype(jnp.int32),
    ])
    left, shift, row = pl.pallas_call(
        lambda *refs: terms_kernel(count, *refs),
        in_specs=[smem] + [vmem] * 2,
        out_shape=(
            pltpu.VMEM((2 * C, 4 * C), BF16),
            pltpu.VMEM((2 * C, W), F32),
            pltpu.VMEM((C, W), F32),
        ),
        cost_estimate=cost(4),
        name="terms",
    )(place, near(pay), point_weight)
    rows = lax.all_to_all(row.reshape(C, 1, W), "sample", 0, 0).reshape(C, W)
    white, d_volume = pl.pallas_call(
        grads_kernel,
        in_specs=[smem] + [vmem] * 8,
        out_shape=(shape((C, D, H, W), BF16), shape((C, D, H, W), BF16)),
        scratch_shapes=[
            pltpu.VMEM((D + 2, C, PW), F32),
            pltpu.VMEM((27, C, W), F32),
            pltpu.VMEM((D, C, HW), F32),
        ],
        cost_estimate=cost(8),
        name="grads",
    )(
        place, near(left), near(shift), near(gm_lo), near(gm_first), near(gm_inner),
        near(gm_last), near(gm_hi), depth_kernel,
    )
    return white[None], d_volume[None], rows[:, 0:C].T, rows[:, C : C + 27]


def solution(mesh):
    split = P("sample", None, "space", None, None)
    return jax.shard_map(
        whole_step,
        mesh=mesh,
        in_specs=(split, P(), P(), split),
        out_specs=(split, split, P(), P()),
        check_vma=False,
    )
```

```python
import math

import jax
import jax.numpy as jnp
from jax import lax
from jax.experimental import pallas as pl
from jax.experimental.pallas import tpu as pltpu
from jax.sharding import PartitionSpec as P

NEWTON = 5
EPSILON = 1e-05
C = 32
D = 4
H = 16
W = 128
HW = H * W
PW = (H + 2) * W
ROWS = 24
HIGH = lax.Precision.HIGHEST
F32 = jnp.float32
BF16 = jnp.bfloat16


def dot(a, b, dims=((1,), (0,)), precision=None):
    return lax.dot_general(
        a, b, (dims, ((), ())), precision=precision, preferred_element_type=F32
    )


def dot_high(a, b, dims=((1,), (0,))):
    return dot(a, b, dims, HIGH)


def iota(shape, dim):
    return lax.broadcasted_iota(jnp.int32, shape, dim)


def spread_taps(dk_ref, taps_ref, flip):
    for t in range(27):
        s = 26 - t if flip else t
        taps_ref[t] = jnp.broadcast_to(dk_ref[:, s : s + 1], (C, W))


def stencil(src_ref, taps_ref, dst_ref, planes, step=1):
    lane = iota((8, W), 1)

    def plane(i, carry):
        group = i // planes
        p = i - group * planes
        rows = pl.ds(pl.multiple_of(8 * group, 8), 8)
        taps = [taps_ref[t, rows, :] for t in range(27)]
        for h in range(H):
            parts = [None, None, None]
            for a in range(3):
                for b in range(3):
                    cells = src_ref[step * p + a, rows, (h + b) * W : (h + b + 1) * W]
                    for e in range(3):
                        term = taps[9 * a + 3 * b + e] * cells
                        parts[e] = term if parts[e] is None else parts[e] + term
            left = jnp.where(lane == 0, 0.0, pltpu.roll(parts[0], 1, 1))
            right = jnp.where(lane == W - 1, 0.0, pltpu.roll(parts[2], W - 1, 1))
            dst_ref[p, rows, h * W : (h + 1) * W] = parts[1] + left + right
        return carry

    lax.fori_loop(0, planes * (C // 8), plane, 0)


def slab_sums(xs, gs, step, dk_ref, w_ref, gm_refs, acc_ref,
              xf_ref, xb_ref, hid_ref, taps_ref, right_ref):
    zeros = jnp.zeros((len(xs), C, W), F32)
    xf_ref[:, :, 0:W] = zeros
    xf_ref[:, :, PW - W : PW] = zeros
    xb_ref[:, :, 0:W] = zeros.astype(BF16)
    xb_ref[:, :, PW - W : PW] = zeros.astype(BF16)
    for p, cells in enumerate(xs):
        cells = cells().reshape(C, HW)
        xf_ref[p, :, W : W + HW] = cells.astype(F32)
        xb_ref[p, :, W : W + HW] = cells
    spread_taps(dk_ref, taps_ref, False)
    stencil(xf_ref, taps_ref, hid_ref, 2, step)

    lane = iota((1, W), 1)
    row16 = iota((16, W), 0)
    lane16 = iota((16, W), 1)
    keep0 = (lane < W - 1).astype(F32).astype(BF16)
    keep2 = (lane > 0).astype(F32).astype(BF16)
    ones = jnp.where(
        ((row16 == 0) & (lane16 < W - 1)) | (row16 == 1) | ((row16 == 2) & (lane16 > 0)),
        1.0, 0.0,
    ).astype(BF16)
    for h in range(H):
        right_ref[192:208, h * W : (h + 1) * W] = ones
    first = jnp.where(iota((16, HW), 0) == 0, 1.0, 0.0).astype(BF16)
    for i in range(2):
        hidden = hid_ref[i].astype(BF16)
        mixed = dot(w_ref[...], hidden).astype(BF16)
        gm_refs[i][0:C, :] = gs[i]().reshape(C, HW)
        gm_refs[i][C : 2 * C, :] = mixed
        for h in range(H):
            span = slice(h * W, (h + 1) * W)
            cells = gm_refs[i][:, span]
            right_ref[0:64, span] = pltpu.roll(cells, W - 1, 1) * keep0
            right_ref[64:128, span] = cells
            right_ref[128:192, span] = pltpu.roll(cells, 1, 1) * keep2
        left = [
            xb_ref[step * i + a, :, b * W : b * W + HW] for a in range(3) for b in range(3)
        ]
        left += [hidden, mixed, first]
        acc_ref[:, 0:208] += dot(
            jnp.concatenate(left, axis=0), right_ref[...], ((1,), (1,))
        )


def edges_kernel(x_ref, first_ref, last_ref, sems):
    first = pltpu.make_async_copy(x_ref.at[:, 0], first_ref, sems.at[0])
    last = pltpu.make_async_copy(x_ref.at[:, D - 1], last_ref, sems.at[1])
    first.start()
    last.start()
    first.wait()
    last.wait()


def inner_kernel(x_ref, g_ref, dk_ref, w_ref, gm_ref, acc_ref, *scratch):
    acc_ref[...] = jnp.zeros(acc_ref.shape, F32)
    xs = [lambda p=p: x_ref[:, p] for p in range(D)]
    gs = [lambda p=p: g_ref[:, p] for p in (1, 2)]
    slab_sums(xs, gs, 1, dk_ref, w_ref, (gm_ref.at[0], gm_ref.at[1]), acc_ref, *scratch)


def outer_kernel(x_ref, g_ref, lo_ref, hi_ref, dk_ref, w_ref, part_ref,
                 gm_lo_ref, gm_hi_ref, send_ref, acc_ref, *scratch):
    acc_ref[...] = part_ref[...]
    xs = [lambda: lo_ref[...]] + [lambda p=p: x_ref[:, p] for p in range(D)]
    xs += [lambda: hi_ref[...]]
    gs = [lambda p=p: g_ref[:, p] for p in (0, 3)]
    slab_sums(xs, gs, 3, dk_ref, w_ref, (gm_lo_ref, gm_hi_ref), acc_ref, *scratch)

    def put(row, slab):
        send_ref[pl.ds(row, C, stride=ROWS), :] = slab

    lane = iota((C, W), 1)
    tile1 = [acc_ref[C * i : C * (i + 1), 128:256] for i in range(10)]
    for ab in range(9):
        put(ab, acc_ref[C * ab : C * (ab + 1), 0:128])
    for i in range(4):
        put(9 + i, jnp.where(lane < 64, tile1[i], pltpu.roll(tile1[4 + i], 64, 1)))
    put(13, jnp.where(lane < 64, tile1[8], acc_ref[288:320, 0:128]))
    counts = jnp.broadcast_to(pltpu.roll(acc_ref[352:353, 0:128], 64, 1), (C, W))
    counts = jnp.where(lane < 64, counts, 0.0)
    for ab in range(9):
        own = jnp.where((lane >= 64) & (lane < 67), tile1[ab], 0.0)
        counts = counts + pltpu.roll(own, 3 * ab, 1)
    counts = counts + pltpu.roll(jnp.where(lane == 65, tile1[9], 0.0), 26, 1)
    put(14, counts)
    put(15, jnp.zeros((C, W), F32))
    row = iota((C, W), 0)
    stats = pltpu.roll(acc_ref[320:352, 0:128], 64, 1)
    second = pltpu.roll(stats, 96, 1)
    swapped = jnp.where(lane < 16, pltpu.roll(stats, 112, 1), pltpu.roll(stats, 16, 1))
    mine = (row < 16) == (lane < 16)
    table = jnp.where(lane < C, jnp.where(mine, second, swapped), 0.0)
    packed = table[0:8]
    for q in range(1, 4):
        packed = packed + pltpu.roll(table[8 * q : 8 * q + 8], 32 * q, 1)
    for r in range(8):
        put(16 + r, jnp.broadcast_to(packed[r : r + 1], (C, W)))


def whiten_terms(stats, count):
    gf_row = stats[14:15, 0:C]
    first_row = stats[14:15, C : 2 * C]
    packed = stats[16:24]
    table = jnp.concatenate([pltpu.roll(packed, (W - 32 * q) % W, 1) for q in range(4)], axis=0)
    table = table[:, 0:C]
    row = iota((C, C), 0)
    col = iota((C, C), 1)
    mine = (row < 16) == (col < 16)
    eye = (row == col).astype(F32)
    low = iota((1, C), 1) < 16
    second = jnp.where(mine, table, 0.0)
    other = jnp.concatenate([table[:, 16:32], table[:, 0:16]], axis=1)
    grad_mat = jnp.where(mine, other, 0.0).T

    def column(values):
        return jnp.sum(eye * values, axis=1, keepdims=True)

    def per_group(values):
        left = jnp.sum(jnp.where(low, values, 0.0), axis=1, keepdims=True)
        right = jnp.sum(jnp.where(low, 0.0, values), axis=1, keepdims=True)
        return jnp.where(low, left, right)

    avg = first_row / count
    avg_col = column(avg)
    cov = second / count - jnp.where(mine, avg_col * avg, 0.0) + EPSILON * eye
    trace = per_group(jnp.sum(cov * eye, axis=0, keepdims=True))
    normed = cov / trace
    d_whiten = grad_mat - jnp.where(mine, column(gf_row) * avg, 0.0)

    project = 1.5 * eye - 0.5 * normed
    slope = -0.5 * d_whiten
    for _ in range(NEWTON - 1):
        pair = jnp.concatenate([project, slope], axis=0)
        squares = dot_high(pair, project)
        scaled = dot_high(pair, normed)
        square = squares[0:C]
        d_square = squares[C : 2 * C] + dot_high(project, slope)
        d_scaled = scaled[C : 2 * C] + dot_high(project, d_whiten)
        cubes = dot_high(jnp.concatenate([square, d_square], axis=0), scaled[0:C])
        slope = 1.5 * slope - 0.5 * (cubes[C : 2 * C] + dot_high(square, d_scaled))
        project = 1.5 * project - 0.5 * cubes[0:C]
    root = jnp.sqrt(trace)
    whiten = project / root
    offset_col = jnp.sum(whiten * avg, axis=1, keepdims=True)
    d_normed = slope / root
    d_trace = jnp.sum(-0.5 * d_whiten * whiten - d_normed * normed, axis=0, keepdims=True)
    d_trace = per_group(d_trace) / trace
    d_cov = d_normed / trace + d_trace * eye
    both = d_cov + d_cov.T
    d_avg = -(dot_high(gf_row, whiten) + dot_high(avg, both))
    return whiten, offset_col, both / count, d_avg / count, column


def terms_kernel(count, place_ref, pay_ref, w_ref, left_ref, shift_ref, row_ref):
    stats = jnp.sum(pay_ref[...], axis=0)
    whiten, offset_col, symmetric, d_first, column = whiten_terms(stats, count)
    weight = w_ref[...].astype(F32)
    from_g = dot_high(weight, whiten, ((0,), (1,)))
    from_m = dot_high(weight, symmetric, ((0,), (0,)))
    bias_col = column(dot_high(d_first, weight))
    hidden_mat = jnp.concatenate([from_g, from_m], axis=1)
    full = jnp.concatenate(
        [hidden_mat, jnp.concatenate([jnp.zeros((C, C), F32), whiten], axis=1)], axis=0
    )
    coarse = full.astype(BF16)
    fine = (full - coarse.astype(F32)).astype(BF16)
    left_ref[...] = jnp.concatenate([coarse, fine], axis=1)
    shift_ref[0:C] = jnp.broadcast_to(bias_col, (C, W))
    shift_ref[C : 2 * C] = jnp.broadcast_to(-offset_col, (C, W))

    mine = place_ref[0]
    pick = (iota((C, 1), 0) == mine).astype(F32)
    chosen = jnp.sum(pick * hidden_mat, axis=0, keepdims=True)
    chosen_bias = jnp.sum(pick * bias_col, axis=0, keepdims=True)
    prod = stats[0:16] * jnp.concatenate([chosen, chosen], axis=1)
    lane16 = iota((16, W), 1)
    row16 = iota((16, W), 0)
    low = jnp.sum(jnp.where(lane16 < 64, prod, 0.0), axis=1, keepdims=True)
    high = jnp.sum(jnp.where(lane16 < 64, 0.0, prod), axis=1, keepdims=True)
    to_low = jnp.where(row16 < 9, C + 3 * row16, C + 3 * (row16 - 9) + 2)
    to_low = jnp.where(row16 == 13, C + 26, jnp.where(row16 > 13, -1, to_low))
    to_high = jnp.where(row16 < 9, C + 3 * row16 + 1, C + 3 * (row16 - 5) + 2)
    to_high = jnp.where(row16 > 12, -1, to_high)
    taps_row = jnp.where(lane16 == to_low, low, 0.0) + jnp.where(lane16 == to_high, high, 0.0)
    taps_row = jnp.sum(taps_row, axis=0, keepdims=True)
    lane = iota((1, W), 1)
    ones_row = jnp.where((lane >= 64) & (lane < 91), stats[14:15], 0.0)
    taps_row = taps_row + chosen_bias * pltpu.roll(ones_row, W - 32, 1)
    hidden_sum = jnp.sum(jnp.where(lane == 91, stats[14:15], 0.0), axis=1, keepdims=True)
    pair = pltpu.roll(stats[13:14], 64, 1)[:, 0:64]
    point = dot_high(pair, jnp.concatenate([whiten, symmetric], axis=0)) + hidden_sum * d_first
    point = jnp.concatenate([point, jnp.zeros((1, W - C), F32)], axis=1)
    row = (taps_row + point) * (1.0 / math.sqrt(count))
    row_ref[...] = jnp.broadcast_to(row, (C, W))


def grads_kernel(place_ref, left_ref, shift_ref, lo_ref, first_ref, inner_ref, last_ref, hi_ref,
                 dk_ref, white_ref, dvol_ref, dh_ref, taps_ref, out_ref):
    zeros = jnp.zeros((D + 2, C, W), F32)
    dh_ref[:, :, 0:W] = zeros
    dh_ref[:, :, PW - W : PW] = zeros
    inside_lo = place_ref[1].astype(F32)
    inside_hi = place_ref[2].astype(F32)
    left = left_ref[...]
    bias = shift_ref[0:C, 0:1]
    minus_offset = shift_ref[C : 2 * C, 0:1]
    planes = [lo_ref, first_ref, inner_ref.at[0], inner_ref.at[1], last_ref, hi_ref]
    for p in range(D + 2):
        cells = planes[p][...]
        both = dot(left, jnp.concatenate([cells, cells], axis=0))
        d_hidden = both[0:C] + bias
        if p == 0:
            d_hidden = d_hidden * inside_lo
        elif p > D:
            d_hidden = d_hidden * inside_hi
        else:
            white = (both[C : 2 * C] + minus_offset).astype(BF16)
            white_ref[:, p - 1] = white.reshape(C, H, W)
        dh_ref[p, :, W : W + HW] = d_hidden
    spread_taps(dk_ref, taps_ref, True)
    stencil(dh_ref, taps_ref, out_ref, D)
    for z in range(D):
        dvol_ref[:, z] = out_ref[z].astype(BF16).reshape(C, H, W)


def finish_kernel(rows_ref, point_ref, taps_ref):
    rows = rows_ref[...]
    point_ref[...] = rows[:, 0:C].T
    taps_ref[...] = rows[:, C : C + 27]


def cost(us):
    return pl.CostEstimate(flops=int(us * 1e8), bytes_accessed=int(us * 1e6), transcendentals=0)


def whole_step(volumes, depth_kernel, point_weight, cotangent):
    x = volumes[0]
    g = cotangent[0]
    samples = lax.axis_size("sample")
    slabs = lax.axis_size("space")
    count = float(D * HW * samples * slabs)
    forward = [(i, i + 1) for i in range(slabs - 1)]
    backward = [(i + 1, i) for i in range(slabs - 1)]
    scratch = lambda planes: [
        pltpu.VMEM((planes, C, PW), F32),
        pltpu.VMEM((planes, C, PW), BF16),
        pltpu.VMEM((2, C, HW), F32),
        pltpu.VMEM((27, C, W), F32),
        pltpu.VMEM((208, HW), BF16),
    ]
    vmem = pl.BlockSpec(memory_space=pltpu.VMEM)
    smem = pl.BlockSpec(memory_space=pltpu.SMEM)
    shape = jax.ShapeDtypeStruct
    near = lambda array: pltpu.with_memory_space_constraint(array, pltpu.VMEM)

    x_first, x_last = pl.pallas_call(
        edges_kernel,
        in_specs=[pl.BlockSpec(memory_space=pl.ANY)],
        out_shape=(pltpu.VMEM((C, H, W), BF16), pltpu.VMEM((C, H, W), BF16)),
        scratch_shapes=[pltpu.SemaphoreType.DMA((2,))],
        name="edges",
    )(x)
    x_lo = lax.ppermute(x_last, "space", forward)
    x_hi = lax.ppermute(x_first, "space", backward)
    gm_inner, acc = pl.pallas_call(
        inner_kernel,
        out_shape=(pltpu.VMEM((2, 2 * C, HW), BF16), pltpu.VMEM((368, 256), F32)),
        scratch_shapes=scratch(D),
        cost_estimate=cost(6),
        name="inner",
    )(x, g, depth_kernel, point_weight)
    gm_first, gm_last, send = pl.pallas_call(
        outer_kernel,
        out_shape=(
            pltpu.VMEM((2 * C, HW), BF16),
            pltpu.VMEM((2 * C, HW), BF16),
            pltpu.VMEM((C * ROWS, W), F32),
        ),
        scratch_shapes=[pltpu.VMEM((368, 256), F32)] + scratch(D + 2),
        cost_estimate=cost(6),
        name="outer",
    )(x, g, near(x_lo), near(x_hi), depth_kernel, point_weight, near(acc))
    gm_lo = lax.ppermute(gm_last, "space", forward)
    gm_hi = lax.ppermute(gm_first, "space", backward)
    parts = lax.all_to_all(send.reshape(C, ROWS, W), "sample", 0, 0)
    part = jnp.sum(parts, axis=0)
    pay = lax.all_to_all(jnp.broadcast_to(part, (slabs, ROWS, W)), "space", 0, 0)
    slab = lax.axis_index("space")
    place = jnp.stack([
        lax.axis_index("sample"),
        (slab > 0).astype(jnp.int32),
        (slab < slabs - 1).astype(jnp.int32),
    ])
    left, shift, row = pl.pallas_call(
        lambda *refs: terms_kernel(count, *refs),
        in_specs=[smem] + [vmem] * 2,
        out_shape=(
            pltpu.VMEM((2 * C, 4 * C), BF16),
            pltpu.VMEM((2 * C, W), F32),
            pltpu.VMEM((C, W), F32),
        ),
        cost_estimate=cost(4),
        name="terms",
    )(place, near(pay), point_weight)
    rows = lax.all_to_all(row.reshape(C, 1, W), "sample", 0, 0).reshape(C, W)
    white, d_volume = pl.pallas_call(
        grads_kernel,
        in_specs=[smem] + [vmem] * 8,
        out_shape=(shape((C, D, H, W), BF16), shape((C, D, H, W), BF16)),
        scratch_shapes=[
            pltpu.VMEM((D + 2, C, PW), F32),
            pltpu.VMEM((27, C, W), F32),
            pltpu.VMEM((D, C, HW), F32),
        ],
        cost_estimate=cost(8),
        name="grads",
    )(
        place, near(left), near(shift), near(gm_lo), near(gm_first), near(gm_inner),
        near(gm_last), near(gm_hi), depth_kernel,
    )
    d_point, d_kernel = pl.pallas_call(
        finish_kernel,
        out_shape=(shape((C, C), F32), shape((C, 27), F32)),
        in_specs=[vmem],
        name="finish",
    )(near(rows))
    return white[None], d_volume[None], d_point, d_kernel


def solution(mesh):
    split = P("sample", None, "space", None, None)
    return jax.shard_map(
        whole_step,
        mesh=mesh,
        in_specs=(split, P(), P(), split),
        out_specs=(split, split, P(), P()),
        check_vma=False,
    )
```

```python
import math

import jax
import jax.numpy as jnp
from jax import lax
from jax.experimental import pallas as pl
from jax.experimental.pallas import tpu as pltpu
from jax.sharding import PartitionSpec as P

NEWTON = 5
EPSILON = 1e-05
C = 32
D = 4
H = 16
W = 128
HW = H * W
PW = (H + 2) * W
SPAN = 512
ROWS = 24
HIGH = lax.Precision.HIGHEST
F32 = jnp.float32
BF16 = jnp.bfloat16


def dot(a, b, dims=((1,), (0,)), precision=None):
    return lax.dot_general(
        a, b, (dims, ((), ())), precision=precision, preferred_element_type=F32
    )


def dot_high(a, b, dims=((1,), (0,))):
    return dot(a, b, dims, HIGH)


def iota(shape, dim):
    return lax.broadcasted_iota(jnp.int32, shape, dim)


def two_terms(values):
    coarse = values.astype(BF16)
    return coarse, (values - coarse.astype(F32)).astype(BF16)


def tap_matrices(dk_ref, flip):
    row = iota((C, W), 0)
    lane = iota((C, W), 1)
    taps = [
        jnp.broadcast_to(dk_ref[:, (26 - t if flip else t) : (27 - t if flip else t + 1)], (C, W))
        for t in range(27)
    ]
    blocks = []
    for e in range(3):
        halves = []
        for half in range(2):
            block = jnp.zeros((C, W), F32)
            for i in range(4):
                block = jnp.where(lane == row + C * i, taps[3 * (4 * half + i) + e], block)
            halves.append(block)
        blocks.append(jnp.concatenate(halves, axis=1))
    return jnp.concatenate(blocks, axis=0), taps[24:27]


def stencil_rows(sums, last, last_taps):
    lane = iota((C, W), 1)
    rows = []
    for i in range(last.shape[1] // W):
        span = slice(i * W, (i + 1) * W)
        parts = [sums[C * e : C * (e + 1), span] + last_taps[e] * last[:, span] for e in range(3)]
        left = jnp.where(lane == 0, 0.0, pltpu.roll(parts[0], 1, 1))
        right = jnp.where(lane == W - 1, 0.0, pltpu.roll(parts[2], W - 1, 1))
        rows.append(parts[1] + left + right)
    return jnp.concatenate(rows, axis=1)


def offsets(ref, plane, start, width):
    return [
        ref[plane + a, :, start + b * W : start + b * W + width]
        for a in range(3) for b in range(3)
    ]


def slab_sums(xs, gs, step, dk_ref, w_ref, gm_refs, acc_ref,
              xb_ref, hid_ref, right_ref):
    zeros = jnp.zeros((len(xs), C, W), F32)
    xb_ref[:, :, 0:W] = zeros.astype(BF16)
    xb_ref[:, :, PW - W : PW] = zeros.astype(BF16)
    for p, cells in enumerate(xs):
        xb_ref[p, :, W : W + HW] = cells().reshape(C, HW)
    matrix, last_taps = tap_matrices(dk_ref, False)
    matrix = jnp.concatenate(two_terms(matrix), axis=0)
    for i in range(2):
        for start in range(0, HW, SPAN):
            cells = offsets(xb_ref, step * i, start, SPAN)
            both = dot(matrix, jnp.concatenate(cells[:8], axis=0))
            rows = stencil_rows(both[:96] + both[96:], cells[8].astype(F32), last_taps)
            hid_ref[i, :, start : start + SPAN] = rows.astype(BF16)

    lane = iota((1, W), 1)
    row16 = iota((16, W), 0)
    lane16 = iota((16, W), 1)
    keep0 = (lane < W - 1).astype(F32).astype(BF16)
    keep2 = (lane > 0).astype(F32).astype(BF16)
    ones = jnp.where(
        ((row16 == 0) & (lane16 < W - 1)) | (row16 == 1) | ((row16 == 2) & (lane16 > 0)),
        1.0, 0.0,
    ).astype(BF16)
    for h in range(H):
        right_ref[192:208, h * W : (h + 1) * W] = ones
    first = jnp.where(iota((16, HW), 0) == 0, 1.0, 0.0).astype(BF16)
    for i in range(2):
        hidden = hid_ref[i]
        mixed = dot(w_ref[...], hidden).astype(BF16)
        gm_refs[i][0:C, :] = gs[i]().reshape(C, HW)
        gm_refs[i][C : 2 * C, :] = mixed
        for h in range(H):
            span = slice(h * W, (h + 1) * W)
            cells = gm_refs[i][:, span]
            right_ref[0:64, span] = pltpu.roll(cells, W - 1, 1) * keep0
            right_ref[64:128, span] = cells
            right_ref[128:192, span] = pltpu.roll(cells, 1, 1) * keep2
        left = offsets(xb_ref, step * i, 0, HW) + [hidden, mixed, first]
        acc_ref[:, 0:208] += dot(
            jnp.concatenate(left, axis=0), right_ref[...], ((1,), (1,))
        )


def edges_kernel(x_ref, near_ref, far_ref, sems):
    even = lax.rem(lax.axis_index("space"), 2) == 0
    plane = jnp.where(even, D - 1, 0)
    first = pltpu.make_async_copy(x_ref.at[:, plane], near_ref, sems.at[0])
    last = pltpu.make_async_copy(x_ref.at[:, D - 1 - plane], far_ref, sems.at[1])
    first.start()
    last.start()
    first.wait()
    last.wait()


def inner_kernel(x_ref, g_ref, dk_ref, w_ref, gm_ref, acc_ref, *scratch):
    acc_ref[...] = jnp.zeros(acc_ref.shape, F32)
    xs = [lambda p=p: x_ref[:, p] for p in range(D)]
    gs = [lambda p=p: g_ref[:, p] for p in (1, 2)]
    slab_sums(xs, gs, 1, dk_ref, w_ref, (gm_ref.at[0], gm_ref.at[1]), acc_ref, *scratch)


def outer_kernel(x_ref, g_ref, near_ref, far_ref, dk_ref, w_ref, part_ref,
                 gm_lo_ref, gm_hi_ref, send_ref, acc_ref, *scratch):
    acc_ref[...] = part_ref[...]
    even = lax.rem(lax.axis_index("space"), 2) == 0
    xs = [lambda: jnp.where(even, far_ref[...], near_ref[...])]
    xs += [lambda p=p: x_ref[:, p] for p in range(D)]
    xs += [lambda: jnp.where(even, near_ref[...], far_ref[...])]
    gs = [lambda p=p: g_ref[:, p] for p in (0, 3)]
    slab_sums(xs, gs, 3, dk_ref, w_ref, (gm_lo_ref, gm_hi_ref), acc_ref, *scratch)

    def put(row, slab):
        send_ref[pl.ds(row, C, stride=ROWS), :] = slab

    lane = iota((C, W), 1)
    tile1 = [acc_ref[C * i : C * (i + 1), 128:256] for i in range(10)]
    for ab in range(9):
        put(ab, acc_ref[C * ab : C * (ab + 1), 0:128])
    for i in range(4):
        put(9 + i, jnp.where(lane < 64, tile1[i], pltpu.roll(tile1[4 + i], 64, 1)))
    put(13, jnp.where(lane < 64, tile1[8], acc_ref[288:320, 0:128]))
    counts = jnp.broadcast_to(pltpu.roll(acc_ref[352:353, 0:128], 64, 1), (C, W))
    counts = jnp.where(lane < 64, counts, 0.0)
    for ab in range(9):
        own = jnp.where((lane >= 64) & (lane < 67), tile1[ab], 0.0)
        counts = counts + pltpu.roll(own, 3 * ab, 1)
    counts = counts + pltpu.roll(jnp.where(lane == 65, tile1[9], 0.0), 26, 1)
    put(14, counts)
    put(15, jnp.zeros((C, W), F32))
    row = iota((C, W), 0)
    stats = pltpu.roll(acc_ref[320:352, 0:128], 64, 1)
    second = pltpu.roll(stats, 96, 1)
    swapped = jnp.where(lane < 16, pltpu.roll(stats, 112, 1), pltpu.roll(stats, 16, 1))
    mine = (row < 16) == (lane < 16)
    table = jnp.where(lane < C, jnp.where(mine, second, swapped), 0.0)
    packed = table[0:8]
    for q in range(1, 4):
        packed = packed + pltpu.roll(table[8 * q : 8 * q + 8], 32 * q, 1)
    for r in range(8):
        put(16 + r, jnp.broadcast_to(packed[r : r + 1], (C, W)))


def whiten_terms(stats, count):
    gf_row = stats[14:15, 0:C]
    first_row = stats[14:15, C : 2 * C]
    packed = stats[16:24]
    table = jnp.concatenate([pltpu.roll(packed, (W - 32 * q) % W, 1) for q in range(4)], axis=0)
    table = table[:, 0:C]
    row = iota((C, C), 0)
    col = iota((C, C), 1)
    mine = (row < 16) == (col < 16)
    eye = (row == col).astype(F32)
    low = iota((1, C), 1) < 16
    second = jnp.where(mine, table, 0.0)
    other = jnp.concatenate([table[:, 16:32], table[:, 0:16]], axis=1)
    grad_mat = jnp.where(mine, other, 0.0).T

    def column(values):
        return jnp.sum(eye * values, axis=1, keepdims=True)

    def per_group(values):
        left = jnp.sum(jnp.where(low, values, 0.0), axis=1, keepdims=True)
        right = jnp.sum(jnp.where(low, 0.0, values), axis=1, keepdims=True)
        return jnp.where(low, left, right)

    avg = first_row / count
    avg_col = column(avg)
    cov = second / count - jnp.where(mine, avg_col * avg, 0.0) + EPSILON * eye
    trace = per_group(jnp.sum(cov * eye, axis=0, keepdims=True))
    normed = cov / trace
    d_whiten = grad_mat - jnp.where(mine, column(gf_row) * avg, 0.0)

    project = 1.5 * eye - 0.5 * normed
    slope = -0.5 * d_whiten
    for _ in range(NEWTON - 1):
        pair = jnp.concatenate([project, slope], axis=0)
        squares = dot_high(pair, project)
        scaled = dot_high(pair, normed)
        square = squares[0:C]
        d_square = squares[C : 2 * C] + dot_high(project, slope)
        d_scaled = scaled[C : 2 * C] + dot_high(project, d_whiten)
        cubes = dot_high(jnp.concatenate([square, d_square], axis=0), scaled[0:C])
        slope = 1.5 * slope - 0.5 * (cubes[C : 2 * C] + dot_high(square, d_scaled))
        project = 1.5 * project - 0.5 * cubes[0:C]
    root = jnp.sqrt(trace)
    whiten = project / root
    offset_col = jnp.sum(whiten * avg, axis=1, keepdims=True)
    d_normed = slope / root
    d_trace = jnp.sum(-0.5 * d_whiten * whiten - d_normed * normed, axis=0, keepdims=True)
    d_trace = per_group(d_trace) / trace
    d_cov = d_normed / trace + d_trace * eye
    both = d_cov + d_cov.T
    d_avg = -(dot_high(gf_row, whiten) + dot_high(avg, both))
    return whiten, offset_col, both / count, d_avg / count, column


def terms_kernel(count, place_ref, pay_ref, w_ref, left_ref, shift_ref, row_ref):
    stats = jnp.sum(pay_ref[...], axis=0)
    whiten, offset_col, symmetric, d_first, column = whiten_terms(stats, count)
    weight = w_ref[...].astype(F32)
    from_g = dot_high(weight, whiten, ((0,), (1,)))
    from_m = dot_high(weight, symmetric, ((0,), (0,)))
    bias_col = column(dot_high(d_first, weight))
    hidden_mat = jnp.concatenate([from_g, from_m], axis=1)
    full = jnp.concatenate(
        [hidden_mat, jnp.concatenate([jnp.zeros((C, C), F32), whiten], axis=1)], axis=0
    )
    coarse = full.astype(BF16)
    fine = (full - coarse.astype(F32)).astype(BF16)
    left_ref[...] = jnp.concatenate([coarse, fine], axis=1)
    shift_ref[0:C] = jnp.broadcast_to(bias_col, (C, W))
    shift_ref[C : 2 * C] = jnp.broadcast_to(-offset_col, (C, W))

    mine = place_ref[0]
    pick = (iota((C, 1), 0) == mine).astype(F32)
    chosen = jnp.sum(pick * hidden_mat, axis=0, keepdims=True)
    chosen_bias = jnp.sum(pick * bias_col, axis=0, keepdims=True)
    prod = stats[0:16] * jnp.concatenate([chosen, chosen], axis=1)
    lane16 = iota((16, W), 1)
    row16 = iota((16, W), 0)
    low = jnp.sum(jnp.where(lane16 < 64, prod, 0.0), axis=1, keepdims=True)
    high = jnp.sum(jnp.where(lane16 < 64, 0.0, prod), axis=1, keepdims=True)
    to_low = jnp.where(row16 < 9, C + 3 * row16, C + 3 * (row16 - 9) + 2)
    to_low = jnp.where(row16 == 13, C + 26, jnp.where(row16 > 13, -1, to_low))
    to_high = jnp.where(row16 < 9, C + 3 * row16 + 1, C + 3 * (row16 - 5) + 2)
    to_high = jnp.where(row16 > 12, -1, to_high)
    taps_row = jnp.where(lane16 == to_low, low, 0.0) + jnp.where(lane16 == to_high, high, 0.0)
    taps_row = jnp.sum(taps_row, axis=0, keepdims=True)
    lane = iota((1, W), 1)
    ones_row = jnp.where((lane >= 64) & (lane < 91), stats[14:15], 0.0)
    taps_row = taps_row + chosen_bias * pltpu.roll(ones_row, W - 32, 1)
    hidden_sum = jnp.sum(jnp.where(lane == 91, stats[14:15], 0.0), axis=1, keepdims=True)
    pair = pltpu.roll(stats[13:14], 64, 1)[:, 0:64]
    point = dot_high(pair, jnp.concatenate([whiten, symmetric], axis=0)) + hidden_sum * d_first
    point = jnp.concatenate([point, jnp.zeros((1, W - C), F32)], axis=1)
    row = (taps_row + point) * (1.0 / math.sqrt(count))
    row_ref[...] = jnp.broadcast_to(row, (C, W))


def grads_kernel(place_ref, left_ref, shift_ref, lo_ref, first_ref, inner_ref, last_ref, hi_ref,
                 dk_ref, white_ref, dvol_ref, coarse_ref, fine_ref, out_ref):
    zeros = jnp.zeros((D + 2, C, W), BF16)
    for ref in (coarse_ref, fine_ref):
        ref[:, :, 0:W] = zeros
        ref[:, :, PW - W : PW] = zeros
    inside_lo = place_ref[1].astype(F32)
    inside_hi = place_ref[2].astype(F32)
    left = left_ref[...]
    bias = shift_ref[0:C, 0:1]
    minus_offset = shift_ref[C : 2 * C, 0:1]
    planes = [lo_ref, first_ref, inner_ref.at[0], inner_ref.at[1], last_ref, hi_ref]
    for p in range(D + 2):
        cells = planes[p][...]
        both = dot(left, jnp.concatenate([cells, cells], axis=0))
        d_hidden = both[0:C] + bias
        if p == 0:
            d_hidden = d_hidden * inside_lo
        elif p > D:
            d_hidden = d_hidden * inside_hi
        else:
            white = (both[C : 2 * C] + minus_offset).astype(BF16)
            white_ref[:, p - 1] = white.reshape(C, H, W)
        terms = two_terms(d_hidden)
        coarse_ref[p, :, W : W + HW] = terms[0]
        fine_ref[p, :, W : W + HW] = terms[1]
    matrix, last_taps = tap_matrices(dk_ref, True)
    terms = two_terms(matrix)
    matrix = jnp.concatenate(terms, axis=0)
    for z in range(D):
        for start in range(0, HW, SPAN):
            coarse = offsets(coarse_ref, z, start, SPAN)
            fine = offsets(fine_ref, z, start, SPAN)
            both = dot(matrix, jnp.concatenate(coarse[:8], axis=0))
            rest = dot(terms[0], jnp.concatenate(fine[:8], axis=0))
            last = coarse[8].astype(F32) + fine[8].astype(F32)
            rows = stencil_rows(both[:96] + both[96:] + rest, last, last_taps)
            out_ref[:, start : start + SPAN] = rows.astype(BF16)
        dvol_ref[:, z] = out_ref[...].reshape(C, H, W)


def finish_kernel(rows_ref, point_ref, taps_ref):
    rows = rows_ref[...]
    point_ref[...] = rows[:, 0:C].T
    taps_ref[...] = rows[:, C : C + 27]


def cost(us):
    return pl.CostEstimate(flops=int(us * 1e8), bytes_accessed=int(us * 1e6), transcendentals=0)


def whole_step(volumes, depth_kernel, point_weight, cotangent):
    x = volumes[0]
    g = cotangent[0]
    samples = lax.axis_size("sample")
    slabs = lax.axis_size("space")
    count = float(D * HW * samples * slabs)
    forward = [(i, i + 1) for i in range(slabs - 1)]
    backward = [(i + 1, i) for i in range(slabs - 1)]
    scratch = lambda planes: [
        pltpu.VMEM((planes, C, PW), BF16),
        pltpu.VMEM((2, C, HW), BF16),
        pltpu.VMEM((208, HW), BF16),
    ]
    vmem = pl.BlockSpec(memory_space=pltpu.VMEM)
    smem = pl.BlockSpec(memory_space=pltpu.SMEM)
    shape = jax.ShapeDtypeStruct
    near = lambda array: pltpu.with_memory_space_constraint(array, pltpu.VMEM)

    near_plane, far_plane = pl.pallas_call(
        edges_kernel,
        in_specs=[pl.BlockSpec(memory_space=pl.ANY)],
        out_shape=(pltpu.VMEM((C, H, W), BF16), pltpu.VMEM((C, H, W), BF16)),
        scratch_shapes=[pltpu.SemaphoreType.DMA((2,))],
        name="edges",
    )(x)
    partners = [(i, i ^ 1) for i in range(slabs) if i ^ 1 < slabs]
    others = [(i, i + 1 if i % 2 else i - 1) for i in range(1, slabs) if i % 2 == 0 or i + 1 < slabs]
    near_plane = lax.ppermute(near_plane, "space", partners)
    far_plane = lax.ppermute(far_plane, "space", others)
    gm_inner, acc = pl.pallas_call(
        inner_kernel,
        out_shape=(pltpu.VMEM((2, 2 * C, HW), BF16), pltpu.VMEM((368, 256), F32)),
        scratch_shapes=scratch(D),
        cost_estimate=cost(6),
        name="inner",
    )(x, g, depth_kernel, point_weight)
    gm_first, gm_last, send = pl.pallas_call(
        outer_kernel,
        out_shape=(
            pltpu.VMEM((2 * C, HW), BF16),
            pltpu.VMEM((2 * C, HW), BF16),
            pltpu.VMEM((C * ROWS, W), F32),
        ),
        scratch_shapes=[pltpu.VMEM((368, 256), F32)] + scratch(D + 2),
        cost_estimate=cost(6),
        name="outer",
    )(x, g, near(near_plane), near(far_plane), depth_kernel, point_weight, near(acc))
    gm_lo = lax.ppermute(gm_last, "space", forward)
    gm_hi = lax.ppermute(gm_first, "space", backward)
    parts = lax.all_to_all(send.reshape(C, ROWS, W), "sample", 0, 0)
    part = jnp.sum(parts, axis=0)
    pay = lax.all_to_all(jnp.broadcast_to(part, (slabs, ROWS, W)), "space", 0, 0)
    slab = lax.axis_index("space")
    place = jnp.stack([
        lax.axis_index("sample"),
        (slab > 0).astype(jnp.int32),
        (slab < slabs - 1).astype(jnp.int32),
    ])
    left, shift, row = pl.pallas_call(
        lambda *refs: terms_kernel(count, *refs),
        in_specs=[smem] + [vmem] * 2,
        out_shape=(
            pltpu.VMEM((2 * C, 4 * C), BF16),
            pltpu.VMEM((2 * C, W), F32),
            pltpu.VMEM((C, W), F32),
        ),
        cost_estimate=cost(4),
        name="terms",
    )(place, near(pay), point_weight)
    rows = lax.all_to_all(row.reshape(C, 1, W), "sample", 0, 0).reshape(C, W)
    white, d_volume = pl.pallas_call(
        grads_kernel,
        in_specs=[smem] + [vmem] * 8,
        out_shape=(shape((C, D, H, W), BF16), shape((C, D, H, W), BF16)),
        scratch_shapes=[
            pltpu.VMEM((D + 2, C, PW), BF16),
            pltpu.VMEM((D + 2, C, PW), BF16),
            pltpu.VMEM((C, HW), BF16),
        ],
        cost_estimate=cost(8),
        name="grads",
    )(
        place, near(left), near(shift), near(gm_lo), near(gm_first), near(gm_inner),
        near(gm_last), near(gm_hi), depth_kernel,
    )
    d_point, d_kernel = pl.pallas_call(
        finish_kernel,
        out_shape=(shape((C, C), F32), shape((C, 27), F32)),
        in_specs=[vmem],
        name="finish",
    )(near(rows))
    return white[None], d_volume[None], d_point, d_kernel


def solution(mesh):
    split = P("sample", None, "space", None, None)
    return jax.shard_map(
        whole_step,
        mesh=mesh,
        in_specs=(split, P(), P(), split),
        out_specs=(split, split, P(), P()),
        check_vma=False,
    )
```

```python
import math

import jax
import jax.numpy as jnp
from jax import lax
from jax.experimental import pallas as pl
from jax.experimental.pallas import tpu as pltpu
from jax.sharding import PartitionSpec as P


NEWTON = 5
EPSILON = 1e-05
C = 32
D = 4
H = 16
W = 128
HW = H * W
PW = (H + 2) * W
SPAN = 512
ROWS = 24
HIGH = lax.Precision.HIGHEST
F32 = jnp.float32
BF16 = jnp.bfloat16


def dot(a, b, dims=((1,), (0,)), precision=None):
    return lax.dot_general(
        a, b, (dims, ((), ())), precision=precision, preferred_element_type=F32
    )


def dot_high(a, b, dims=((1,), (0,))):
    return dot(a, b, dims, HIGH)


def iota(shape, dim):
    return lax.broadcasted_iota(jnp.int32, shape, dim)


def two_terms(values):
    coarse = values.astype(BF16)
    return coarse, (values - coarse.astype(F32)).astype(BF16)


def tap_matrices(dk_ref, flip):
    row = iota((C, W), 0)
    lane = iota((C, W), 1)
    taps = [
        jnp.broadcast_to(dk_ref[:, (26 - t if flip else t) : (27 - t if flip else t + 1)], (C, W))
        for t in range(27)
    ]
    blocks = []
    for e in range(3):
        halves = []
        for half in range(2):
            block = jnp.zeros((C, W), F32)
            for i in range(4):
                block = jnp.where(lane == row + C * i, taps[3 * (4 * half + i) + e], block)
            halves.append(block)
        blocks.append(jnp.concatenate(halves, axis=1))
    return jnp.concatenate(blocks, axis=0), taps[24:27]


def stencil_rows(sums, last, last_taps):
    lane = iota((C, W), 1)
    rows = []
    for i in range(last.shape[1] // W):
        span = slice(i * W, (i + 1) * W)
        parts = [sums[C * e : C * (e + 1), span] + last_taps[e] * last[:, span] for e in range(3)]
        left = jnp.where(lane == 0, 0.0, pltpu.roll(parts[0], 1, 1))
        right = jnp.where(lane == W - 1, 0.0, pltpu.roll(parts[2], W - 1, 1))
        rows.append(parts[1] + left + right)
    return jnp.concatenate(rows, axis=1)


def offsets(planes, start, width):
    return [
        planes[a][:, start + b * W : start + b * W + width] for a in range(3) for b in range(3)
    ]


def fill_plane(ref, cells):
    zeros = jnp.zeros((C, W), BF16)
    ref[:, 0:W] = zeros
    ref[:, PW - W : PW] = zeros
    ref[:, W : W + HW] = cells.reshape(C, HW)


def slab_sums(triples, gs, dk_ref, w_ref, gm_refs, acc_ref, hid_ref, right_ref):
    matrix, last_taps = tap_matrices(dk_ref, False)
    matrix = jnp.concatenate(two_terms(matrix), axis=0)
    for i in range(2):
        for start in range(0, HW, SPAN):
            cells = offsets(triples[i], start, SPAN)
            both = dot(matrix, jnp.concatenate(cells[:8], axis=0))
            rows = stencil_rows(both[:96] + both[96:], cells[8].astype(F32), last_taps)
            hid_ref[i, :, start : start + SPAN] = rows.astype(BF16)

    lane = iota((1, W), 1)
    row16 = iota((16, W), 0)
    lane16 = iota((16, W), 1)
    keep0 = (lane < W - 1).astype(F32).astype(BF16)
    keep2 = (lane > 0).astype(F32).astype(BF16)
    ones = jnp.where(
        ((row16 == 0) & (lane16 < W - 1)) | (row16 == 1) | ((row16 == 2) & (lane16 > 0)),
        1.0, 0.0,
    ).astype(BF16)
    for h in range(H):
        right_ref[192:208, h * W : (h + 1) * W] = ones
    first = jnp.where(iota((16, HW), 0) == 0, 1.0, 0.0).astype(BF16)
    for i in range(2):
        hidden = hid_ref[i]
        mixed = dot(w_ref[...], hidden).astype(BF16)
        gm_refs[i][0:C, :] = gs[i]()
        gm_refs[i][C : 2 * C, :] = mixed
        for h in range(H):
            span = slice(h * W, (h + 1) * W)
            cells = gm_refs[i][:, span]
            right_ref[0:64, span] = pltpu.roll(cells, W - 1, 1) * keep0
            right_ref[64:128, span] = cells
            right_ref[128:192, span] = pltpu.roll(cells, 1, 1) * keep2
        left = offsets(triples[i], 0, HW) + [hidden, mixed, first]
        acc_ref[:, 0:208] += dot(
            jnp.concatenate(left, axis=0), right_ref[...], ((1,), (1,))
        )


def edges_kernel(x_ref, near_ref, far_ref, sems):
    even = lax.rem(lax.axis_index("space"), 2) == 0
    plane = jnp.where(even, D - 1, 0)
    first = pltpu.make_async_copy(x_ref.at[:, plane], near_ref, sems.at[0])
    last = pltpu.make_async_copy(x_ref.at[:, D - 1 - plane], far_ref, sems.at[1])
    first.start()
    last.start()
    first.wait()
    last.wait()


def inner_kernel(x_ref, g_ref, dk_ref, w_ref, gm_ref, acc_ref, own_ref, edge_ref, *scratch):
    acc_ref[...] = jnp.zeros(acc_ref.shape, F32)
    for p in range(D):
        fill_plane(own_ref.at[p], x_ref[:, p])
    for i, p in enumerate((0, D - 1)):
        edge_ref[i] = g_ref[:, p].reshape(C, HW)
    triples = [[own_ref.at[i + a] for a in range(3)] for i in range(2)]
    gs = [lambda p=p: g_ref[:, p].reshape(C, HW) for p in (1, 2)]
    slab_sums(triples, gs, dk_ref, w_ref, (gm_ref.at[0], gm_ref.at[1]), acc_ref, *scratch)


def outer_kernel(own_ref, edge_ref, near_ref, far_ref, dk_ref, w_ref, part_ref,
                 gm_lo_ref, gm_hi_ref, send_ref, acc_ref, halo_ref, *scratch):
    acc_ref[...] = part_ref[...]
    even = lax.rem(lax.axis_index("space"), 2) == 0
    fill_plane(halo_ref.at[0], jnp.where(even, far_ref[...], near_ref[...]))
    fill_plane(halo_ref.at[1], jnp.where(even, near_ref[...], far_ref[...]))
    triples = [
        [halo_ref.at[0], own_ref.at[0], own_ref.at[1]],
        [own_ref.at[2], own_ref.at[3], halo_ref.at[1]],
    ]
    gs = [lambda i=i: edge_ref[i] for i in range(2)]
    slab_sums(triples, gs, dk_ref, w_ref, (gm_lo_ref, gm_hi_ref), acc_ref, *scratch)

    def put(row, slab):
        send_ref[pl.ds(row, C, stride=ROWS), :] = slab

    lane = iota((C, W), 1)
    tile1 = [acc_ref[C * i : C * (i + 1), 128:256] for i in range(10)]
    for ab in range(9):
        put(ab, acc_ref[C * ab : C * (ab + 1), 0:128])
    for i in range(4):
        put(9 + i, jnp.where(lane < 64, tile1[i], pltpu.roll(tile1[4 + i], 64, 1)))
    put(13, jnp.where(lane < 64, tile1[8], acc_ref[288:320, 0:128]))
    counts = jnp.broadcast_to(pltpu.roll(acc_ref[352:353, 0:128], 64, 1), (C, W))
    counts = jnp.where(lane < 64, counts, 0.0)
    for ab in range(9):
        own = jnp.where((lane >= 64) & (lane < 67), tile1[ab], 0.0)
        counts = counts + pltpu.roll(own, 3 * ab, 1)
    counts = counts + pltpu.roll(jnp.where(lane == 65, tile1[9], 0.0), 26, 1)
    put(14, counts)
    put(15, jnp.zeros((C, W), F32))
    row = iota((C, W), 0)
    stats = pltpu.roll(acc_ref[320:352, 0:128], 64, 1)
    second = pltpu.roll(stats, 96, 1)
    swapped = jnp.where(lane < 16, pltpu.roll(stats, 112, 1), pltpu.roll(stats, 16, 1))
    mine = (row < 16) == (lane < 16)
    table = jnp.where(lane < C, jnp.where(mine, second, swapped), 0.0)
    packed = table[0:8]
    for q in range(1, 4):
        packed = packed + pltpu.roll(table[8 * q : 8 * q + 8], 32 * q, 1)
    for r in range(8):
        put(16 + r, jnp.broadcast_to(packed[r : r + 1], (C, W)))


def whiten_terms(stats, count):
    gf_row = stats[14:15, 0:C]
    first_row = stats[14:15, C : 2 * C]
    packed = stats[16:24]
    table = jnp.concatenate([pltpu.roll(packed, (W - 32 * q) % W, 1) for q in range(4)], axis=0)
    table = table[:, 0:C]
    row = iota((C, C), 0)
    col = iota((C, C), 1)
    mine = (row < 16) == (col < 16)
    eye = (row == col).astype(F32)
    low = iota((1, C), 1) < 16
    second = jnp.where(mine, table, 0.0)
    other = jnp.concatenate([table[:, 16:32], table[:, 0:16]], axis=1)
    grad_mat = jnp.where(mine, other, 0.0).T

    def column(values):
        return jnp.sum(eye * values, axis=1, keepdims=True)

    def per_group(values):
        left = jnp.sum(jnp.where(low, values, 0.0), axis=1, keepdims=True)
        right = jnp.sum(jnp.where(low, 0.0, values), axis=1, keepdims=True)
        return jnp.where(low, left, right)

    avg = first_row / count
    avg_col = column(avg)
    cov = second / count - jnp.where(mine, avg_col * avg, 0.0) + EPSILON * eye
    trace = per_group(jnp.sum(cov * eye, axis=0, keepdims=True))
    normed = cov / trace
    d_whiten = grad_mat - jnp.where(mine, column(gf_row) * avg, 0.0)

    project = 1.5 * eye - 0.5 * normed
    slope = -0.5 * d_whiten
    for _ in range(NEWTON - 1):
        pair = jnp.concatenate([project, slope], axis=0)
        squares = dot_high(pair, project)
        scaled = dot_high(pair, normed)
        square = squares[0:C]
        d_square = squares[C : 2 * C] + dot_high(project, slope)
        d_scaled = scaled[C : 2 * C] + dot_high(project, d_whiten)
        cubes = dot_high(jnp.concatenate([square, d_square], axis=0), scaled[0:C])
        slope = 1.5 * slope - 0.5 * (cubes[C : 2 * C] + dot_high(square, d_scaled))
        project = 1.5 * project - 0.5 * cubes[0:C]
    root = jnp.sqrt(trace)
    whiten = project / root
    offset_col = jnp.sum(whiten * avg, axis=1, keepdims=True)
    d_normed = slope / root
    d_trace = jnp.sum(-0.5 * d_whiten * whiten - d_normed * normed, axis=0, keepdims=True)
    d_trace = per_group(d_trace) / trace
    d_cov = d_normed / trace + d_trace * eye
    both = d_cov + d_cov.T
    d_avg = -(dot_high(gf_row, whiten) + dot_high(avg, both))
    return whiten, offset_col, both / count, d_avg / count, column


def terms_kernel(count, place_ref, pay_ref, w_ref, left_ref, shift_ref, row_ref):
    stats = jnp.sum(pay_ref[...], axis=0)
    whiten, offset_col, symmetric, d_first, column = whiten_terms(stats, count)
    weight = w_ref[...].astype(F32)
    from_g = dot_high(weight, whiten, ((0,), (1,)))
    from_m = dot_high(weight, symmetric, ((0,), (0,)))
    bias_col = column(dot_high(d_first, weight))
    hidden_mat = jnp.concatenate([from_g, from_m], axis=1)
    full = jnp.concatenate(
        [hidden_mat, jnp.concatenate([jnp.zeros((C, C), F32), whiten], axis=1)], axis=0
    )
    coarse = full.astype(BF16)
    fine = (full - coarse.astype(F32)).astype(BF16)
    left_ref[...] = jnp.concatenate([coarse, fine], axis=1)
    shift_ref[0:C] = jnp.broadcast_to(bias_col, (C, W))
    shift_ref[C : 2 * C] = jnp.broadcast_to(-offset_col, (C, W))

    mine = place_ref[0]
    pick = (iota((C, 1), 0) == mine).astype(F32)
    chosen = jnp.sum(pick * hidden_mat, axis=0, keepdims=True)
    chosen_bias = jnp.sum(pick * bias_col, axis=0, keepdims=True)
    prod = stats[0:16] * jnp.concatenate([chosen, chosen], axis=1)
    lane16 = iota((16, W), 1)
    row16 = iota((16, W), 0)
    low = jnp.sum(jnp.where(lane16 < 64, prod, 0.0), axis=1, keepdims=True)
    high = jnp.sum(jnp.where(lane16 < 64, 0.0, prod), axis=1, keepdims=True)
    to_low = jnp.where(row16 < 9, C + 3 * row16, C + 3 * (row16 - 9) + 2)
    to_low = jnp.where(row16 == 13, C + 26, jnp.where(row16 > 13, -1, to_low))
    to_high = jnp.where(row16 < 9, C + 3 * row16 + 1, C + 3 * (row16 - 5) + 2)
    to_high = jnp.where(row16 > 12, -1, to_high)
    taps_row = jnp.where(lane16 == to_low, low, 0.0) + jnp.where(lane16 == to_high, high, 0.0)
    taps_row = jnp.sum(taps_row, axis=0, keepdims=True)
    lane = iota((1, W), 1)
    ones_row = jnp.where((lane >= 64) & (lane < 91), stats[14:15], 0.0)
    taps_row = taps_row + chosen_bias * pltpu.roll(ones_row, W - 32, 1)
    hidden_sum = jnp.sum(jnp.where(lane == 91, stats[14:15], 0.0), axis=1, keepdims=True)
    pair = pltpu.roll(stats[13:14], 64, 1)[:, 0:64]
    point = dot_high(pair, jnp.concatenate([whiten, symmetric], axis=0)) + hidden_sum * d_first
    point = jnp.concatenate([point, jnp.zeros((1, W - C), F32)], axis=1)
    row = (taps_row + point) * (1.0 / math.sqrt(count))
    row_ref[...] = jnp.broadcast_to(row, (C, W))


def grads_kernel(place_ref, left_ref, shift_ref, lo_ref, first_ref, inner_ref, last_ref, hi_ref,
                 dk_ref, white_ref, dvol_ref, coarse_ref, fine_ref, out_ref):
    zeros = jnp.zeros((D + 2, C, W), BF16)
    for ref in (coarse_ref, fine_ref):
        ref[:, :, 0:W] = zeros
        ref[:, :, PW - W : PW] = zeros
    inside_lo = place_ref[1].astype(F32)
    inside_hi = place_ref[2].astype(F32)
    left = left_ref[...]
    bias = shift_ref[0:C, 0:1]
    minus_offset = shift_ref[C : 2 * C, 0:1]
    planes = [lo_ref, first_ref, inner_ref.at[0], inner_ref.at[1], last_ref, hi_ref]
    for p in range(D + 2):
        cells = planes[p][...]
        both = dot(left, jnp.concatenate([cells, cells], axis=0))
        d_hidden = both[0:C] + bias
        if p == 0:
            d_hidden = d_hidden * inside_lo
        elif p > D:
            d_hidden = d_hidden * inside_hi
        else:
            white = (both[C : 2 * C] + minus_offset).astype(BF16)
            white_ref[:, p - 1] = white.reshape(C, H, W)
        terms = two_terms(d_hidden)
        coarse_ref[p, :, W : W + HW] = terms[0]
        fine_ref[p, :, W : W + HW] = terms[1]
    matrix, last_taps = tap_matrices(dk_ref, True)
    terms = two_terms(matrix)
    matrix = jnp.concatenate(terms, axis=0)
    for z in range(D):
        for start in range(0, HW, SPAN):
            coarse = offsets([coarse_ref.at[z + a] for a in range(3)], start, SPAN)
            fine = offsets([fine_ref.at[z + a] for a in range(3)], start, SPAN)
            both = dot(matrix, jnp.concatenate(coarse[:8], axis=0))
            rest = dot(terms[0], jnp.concatenate(fine[:8], axis=0))
            last = coarse[8].astype(F32) + fine[8].astype(F32)
            rows = stencil_rows(both[:96] + both[96:] + rest, last, last_taps)
            out_ref[:, start : start + SPAN] = rows.astype(BF16)
        dvol_ref[:, z] = out_ref[...].reshape(C, H, W)


def finish_kernel(rows_ref, point_ref, taps_ref):
    rows = rows_ref[...]
    point_ref[...] = rows[:, 0:C].T
    taps_ref[...] = rows[:, C : C + 27]


def cost(us):
    return pl.CostEstimate(flops=int(us * 1e8), bytes_accessed=int(us * 1e6), transcendentals=0)


def whole_step(volumes, depth_kernel, point_weight, cotangent):
    x = volumes[0]
    g = cotangent[0]
    samples = lax.axis_size("sample")
    slabs = lax.axis_size("space")
    count = float(D * HW * samples * slabs)
    forward = [(i, i + 1) for i in range(slabs - 1)]
    backward = [(i + 1, i) for i in range(slabs - 1)]
    scratch = [pltpu.VMEM((2, C, HW), BF16), pltpu.VMEM((208, HW), BF16)]
    vmem = pl.BlockSpec(memory_space=pltpu.VMEM)
    smem = pl.BlockSpec(memory_space=pltpu.SMEM)
    shape = jax.ShapeDtypeStruct
    near = lambda array: pltpu.with_memory_space_constraint(array, pltpu.VMEM)

    near_plane, far_plane = pl.pallas_call(
        edges_kernel,
        in_specs=[pl.BlockSpec(memory_space=pl.ANY)],
        out_shape=(pltpu.VMEM((C, H, W), BF16), pltpu.VMEM((C, H, W), BF16)),
        scratch_shapes=[pltpu.SemaphoreType.DMA((2,))],
        name="edges",
    )(x)
    partners = [(i, i ^ 1) for i in range(slabs) if i ^ 1 < slabs]
    others = [(i, i + 1 if i % 2 else i - 1) for i in range(1, slabs) if i % 2 == 0 or i + 1 < slabs]
    near_plane = lax.ppermute(near_plane, "space", partners)
    far_plane = lax.ppermute(far_plane, "space", others)
    gm_inner, acc, own, edge = pl.pallas_call(
        inner_kernel,
        out_shape=(
            pltpu.VMEM((2, 2 * C, HW), BF16),
            pltpu.VMEM((368, 256), F32),
            pltpu.VMEM((D, C, PW), BF16),
            pltpu.VMEM((2, C, HW), BF16),
        ),
        scratch_shapes=scratch,
        cost_estimate=cost(6),
        name="inner",
    )(x, g, depth_kernel, point_weight)
    gm_first, gm_last, send = pl.pallas_call(
        outer_kernel,
        out_shape=(
            pltpu.VMEM((2 * C, HW), BF16),
            pltpu.VMEM((2 * C, HW), BF16),
            pltpu.VMEM((C * ROWS, W), F32),
        ),
        scratch_shapes=[pltpu.VMEM((368, 256), F32), pltpu.VMEM((2, C, PW), BF16)] + scratch,
        cost_estimate=cost(6),
        name="outer",
    )(
        near(own), near(edge), near(near_plane), near(far_plane), depth_kernel, point_weight,
        near(acc),
    )
    gm_lo = lax.ppermute(gm_last, "space", forward)
    gm_hi = lax.ppermute(gm_first, "space", backward)
    parts = lax.all_to_all(send.reshape(C, ROWS, W), "sample", 0, 0)
    part = jnp.broadcast_to(jnp.sum(parts, axis=0), (slabs, ROWS, W))
    pay = lax.all_to_all(part, "space", 0, 0)
    slab = lax.axis_index("space")
    place = jnp.stack([
        lax.axis_index("sample"),
        (slab > 0).astype(jnp.int32),
        (slab < slabs - 1).astype(jnp.int32),
    ])
    left, shift, row = pl.pallas_call(
        lambda *refs: terms_kernel(count, *refs),
        in_specs=[smem] + [vmem] * 2,
        out_shape=(
            pltpu.VMEM((2 * C, 4 * C), BF16),
            pltpu.VMEM((2 * C, W), F32),
            pltpu.VMEM((C, W), F32),
        ),
        cost_estimate=cost(4),
        name="terms",
    )(place, near(pay), point_weight)
    rows = lax.all_to_all(row.reshape(C, 1, W), "sample", 0, 0).reshape(C, W)
    white, d_volume = pl.pallas_call(
        grads_kernel,
        in_specs=[smem] + [vmem] * 8,
        out_shape=(shape((C, D, H, W), BF16), shape((C, D, H, W), BF16)),
        scratch_shapes=[
            pltpu.VMEM((D + 2, C, PW), BF16),
            pltpu.VMEM((D + 2, C, PW), BF16),
            pltpu.VMEM((C, HW), BF16),
        ],
        cost_estimate=cost(8),
        name="grads",
    )(
        place, near(left), near(shift), near(gm_lo), near(gm_first), near(gm_inner),
        near(gm_last), near(gm_hi), depth_kernel,
    )
    d_point, d_kernel = pl.pallas_call(
        finish_kernel,
        out_shape=(shape((C, C), F32), shape((C, 27), F32)),
        in_specs=[vmem],
        name="finish",
    )(near(rows))
    return white[None], d_volume[None], d_point, d_kernel


def solution(mesh):
    split = P("sample", None, "space", None, None)
    return jax.shard_map(
        whole_step,
        mesh=mesh,
        in_specs=(split, P(), P(), split),
        out_specs=(split, split, P(), P()),
        check_vma=False,
    )
```

```python
import math

import jax
import jax.numpy as jnp
from jax import lax
from jax.experimental import pallas as pl
from jax.experimental.pallas import tpu as pltpu
from jax.sharding import PartitionSpec as P


NEWTON = 5
EPSILON = 1e-05
C = 32
D = 4
H = 16
W = 128
HW = H * W
PW = (H + 2) * W
SPAN = 512
ROWS = 24
HALF = 7
HIGH = lax.Precision.HIGHEST
F32 = jnp.float32
BF16 = jnp.bfloat16


def dot(a, b, dims=((1,), (0,)), precision=None):
    return lax.dot_general(
        a, b, (dims, ((), ())), precision=precision, preferred_element_type=F32
    )


def dot_high(a, b, dims=((1,), (0,))):
    return dot(a, b, dims, HIGH)


def iota(shape, dim):
    return lax.broadcasted_iota(jnp.int32, shape, dim)


def two_terms(values):
    coarse = values.astype(BF16)
    return coarse, (values - coarse.astype(F32)).astype(BF16)


def tap_matrices(dk_ref, flip):
    row = iota((C, W), 0)
    lane = iota((C, W), 1)
    taps = [
        jnp.broadcast_to(dk_ref[:, (26 - t if flip else t) : (27 - t if flip else t + 1)], (C, W))
        for t in range(27)
    ]
    blocks = []
    for e in range(3):
        halves = []
        for half in range(2):
            block = jnp.zeros((C, W), F32)
            for i in range(4):
                block = jnp.where(lane == row + C * i, taps[3 * (4 * half + i) + e], block)
            halves.append(block)
        blocks.append(jnp.concatenate(halves, axis=1))
    return jnp.concatenate(blocks, axis=0), taps[24:27]


def stencil_rows(sums, last, last_taps):
    lane = iota((C, W), 1)
    rows = []
    for i in range(last.shape[1] // W):
        span = slice(i * W, (i + 1) * W)
        parts = [sums[C * e : C * (e + 1), span] + last_taps[e] * last[:, span] for e in range(3)]
        left = jnp.where(lane == 0, 0.0, pltpu.roll(parts[0], 1, 1))
        right = jnp.where(lane == W - 1, 0.0, pltpu.roll(parts[2], W - 1, 1))
        rows.append(parts[1] + left + right)
    return jnp.concatenate(rows, axis=1)


def offsets(planes, start, width):
    return [
        planes[a][:, start + b * W : start + b * W + width] for a in range(3) for b in range(3)
    ]


def fill_plane(ref, cells):
    zeros = jnp.zeros((C, W), BF16)
    ref[:, 0:W] = zeros
    ref[:, PW - W : PW] = zeros
    ref[:, W : W + HW] = cells.reshape(C, HW)


def slab_sums(triples, gs, dk_ref, w_ref, gm_refs, acc_ref, hid_ref, right_ref):
    matrix, last_taps = tap_matrices(dk_ref, False)
    matrix = jnp.concatenate(two_terms(matrix), axis=0)
    for i in range(2):
        for start in range(0, HW, SPAN):
            cells = offsets(triples[i], start, SPAN)
            both = dot(matrix, jnp.concatenate(cells[:8], axis=0))
            rows = stencil_rows(both[:96] + both[96:], cells[8].astype(F32), last_taps)
            hid_ref[i, :, start : start + SPAN] = rows.astype(BF16)

    lane = iota((1, W), 1)
    row16 = iota((16, W), 0)
    lane16 = iota((16, W), 1)
    keep0 = (lane < W - 1).astype(F32).astype(BF16)
    keep2 = (lane > 0).astype(F32).astype(BF16)
    ones = jnp.where(
        ((row16 == 0) & (lane16 < W - 1)) | (row16 == 1) | ((row16 == 2) & (lane16 > 0)),
        1.0, 0.0,
    ).astype(BF16)
    for h in range(H):
        right_ref[192:208, h * W : (h + 1) * W] = ones
    first = jnp.where(iota((16, HW), 0) == 0, 1.0, 0.0).astype(BF16)
    for i in range(2):
        hidden = hid_ref[i]
        mixed = dot(w_ref[...], hidden).astype(BF16)
        gm_refs[i][0:C, :] = gs[i]()
        gm_refs[i][C : 2 * C, :] = mixed
        for h in range(H):
            span = slice(h * W, (h + 1) * W)
            cells = gm_refs[i][:, span]
            right_ref[0:64, span] = pltpu.roll(cells, W - 1, 1) * keep0
            right_ref[64:128, span] = cells
            right_ref[128:192, span] = pltpu.roll(cells, 1, 1) * keep2
        left = offsets(triples[i], 0, HW) + [hidden, mixed, first]
        acc_ref[:, 0:208] += dot(
            jnp.concatenate(left, axis=0), right_ref[...], ((1,), (1,))
        )


def edges_kernel(x_ref, near_ref, far_ref, sems):
    even = lax.rem(lax.axis_index("space"), 2) == 0
    plane = jnp.where(even, D - 1, 0)
    first = pltpu.make_async_copy(x_ref.at[:, plane], near_ref, sems.at[0])
    last = pltpu.make_async_copy(x_ref.at[:, D - 1 - plane], far_ref, sems.at[1])
    first.start()
    last.start()
    first.wait()
    last.wait()


def inner_kernel(x_ref, g_ref, dk_ref, w_ref, gm_ref, acc_ref, own_ref, edge_ref, *scratch):
    acc_ref[...] = jnp.zeros(acc_ref.shape, F32)
    for p in range(D):
        fill_plane(own_ref.at[p], x_ref[:, p])
    for i, p in enumerate((0, D - 1)):
        edge_ref[i] = g_ref[:, p].reshape(C, HW)
    triples = [[own_ref.at[i + a] for a in range(3)] for i in range(2)]
    gs = [lambda p=p: g_ref[:, p].reshape(C, HW) for p in (1, 2)]
    slab_sums(triples, gs, dk_ref, w_ref, (gm_ref.at[0], gm_ref.at[1]), acc_ref, *scratch)


def outer_kernel(own_ref, edge_ref, near_ref, far_ref, dk_ref, w_ref, part_ref,
                 gm_lo_ref, gm_hi_ref, send_ref, acc_ref, halo_ref, *scratch):
    acc_ref[...] = part_ref[...]
    even = lax.rem(lax.axis_index("space"), 2) == 0
    fill_plane(halo_ref.at[0], jnp.where(even, far_ref[...], near_ref[...]))
    fill_plane(halo_ref.at[1], jnp.where(even, near_ref[...], far_ref[...]))
    triples = [
        [halo_ref.at[0], own_ref.at[0], own_ref.at[1]],
        [own_ref.at[2], own_ref.at[3], halo_ref.at[1]],
    ]
    gs = [lambda i=i: edge_ref[i] for i in range(2)]
    slab_sums(triples, gs, dk_ref, w_ref, (gm_lo_ref, gm_hi_ref), acc_ref, *scratch)

    def put(row, slab):
        send_ref[pl.ds(row, C, stride=ROWS), :] = slab

    lane = iota((C, W), 1)
    tile1 = [acc_ref[C * i : C * (i + 1), 128:256] for i in range(10)]
    for ab in range(9):
        put(ab, acc_ref[C * ab : C * (ab + 1), 0:128])
    for i in range(4):
        put(9 + i, jnp.where(lane < 64, tile1[i], pltpu.roll(tile1[4 + i], 64, 1)))
    put(13, jnp.where(lane < 64, tile1[8], acc_ref[288:320, 0:128]))
    counts = jnp.broadcast_to(pltpu.roll(acc_ref[352:353, 0:128], 64, 1), (C, W))
    counts = jnp.where(lane < 64, counts, 0.0)
    for ab in range(9):
        own = jnp.where((lane >= 64) & (lane < 67), tile1[ab], 0.0)
        counts = counts + pltpu.roll(own, 3 * ab, 1)
    counts = counts + pltpu.roll(jnp.where(lane == 65, tile1[9], 0.0), 26, 1)
    put(14, counts)
    put(23, jnp.zeros((C, W), F32))
    row = iota((C, W), 0)
    stats = pltpu.roll(acc_ref[320:352, 0:128], 64, 1)
    second = pltpu.roll(stats, 96, 1)
    swapped = jnp.where(lane < 16, pltpu.roll(stats, 112, 1), pltpu.roll(stats, 16, 1))
    mine = (row < 16) == (lane < 16)
    table = jnp.where(lane < C, jnp.where(mine, second, swapped), 0.0)
    packed = table[0:8]
    for q in range(1, 4):
        packed = packed + pltpu.roll(table[8 * q : 8 * q + 8], 32 * q, 1)
    for r in range(8):
        put(15 + r, jnp.broadcast_to(packed[r : r + 1], (C, W)))


def fold_kernel(parts_ref, out_ref):
    total = jnp.sum(parts_ref[...], axis=0)
    for slab in range(out_ref.shape[0]):
        half = HALF * (slab % 2)
        out_ref[slab, 0:HALF] = total[half : half + HALF]
        out_ref[slab, HALF : HALF + 9] = total[2 * HALF : 2 * HALF + 9]


def whiten_terms(stats, count):
    gf_row = stats[HALF : HALF + 1, 0:C]
    first_row = stats[HALF : HALF + 1, C : 2 * C]
    packed = stats[HALF + 1 : HALF + 9]
    table = jnp.concatenate([pltpu.roll(packed, (W - 32 * q) % W, 1) for q in range(4)], axis=0)
    table = table[:, 0:C]
    row = iota((C, C), 0)
    col = iota((C, C), 1)
    mine = (row < 16) == (col < 16)
    eye = (row == col).astype(F32)
    low = iota((1, C), 1) < 16
    second = jnp.where(mine, table, 0.0)
    other = jnp.concatenate([table[:, 16:32], table[:, 0:16]], axis=1)
    grad_mat = jnp.where(mine, other, 0.0).T

    def column(values):
        return jnp.sum(eye * values, axis=1, keepdims=True)

    def per_group(values):
        left = jnp.sum(jnp.where(low, values, 0.0), axis=1, keepdims=True)
        right = jnp.sum(jnp.where(low, 0.0, values), axis=1, keepdims=True)
        return jnp.where(low, left, right)

    avg = first_row / count
    avg_col = column(avg)
    cov = second / count - jnp.where(mine, avg_col * avg, 0.0) + EPSILON * eye
    trace = per_group(jnp.sum(cov * eye, axis=0, keepdims=True))
    normed = cov / trace
    d_whiten = grad_mat - jnp.where(mine, column(gf_row) * avg, 0.0)

    project = 1.5 * eye - 0.5 * normed
    slope = -0.5 * d_whiten
    for _ in range(NEWTON - 1):
        pair = jnp.concatenate([project, slope], axis=0)
        squares = dot_high(pair, project)
        scaled = dot_high(pair, normed)
        square = squares[0:C]
        d_square = squares[C : 2 * C] + dot_high(project, slope)
        d_scaled = scaled[C : 2 * C] + dot_high(project, d_whiten)
        cubes = dot_high(jnp.concatenate([square, d_square], axis=0), scaled[0:C])
        slope = 1.5 * slope - 0.5 * (cubes[C : 2 * C] + dot_high(square, d_scaled))
        project = 1.5 * project - 0.5 * cubes[0:C]
    root = jnp.sqrt(trace)
    whiten = project / root
    offset_col = jnp.sum(whiten * avg, axis=1, keepdims=True)
    d_normed = slope / root
    d_trace = jnp.sum(-0.5 * d_whiten * whiten - d_normed * normed, axis=0, keepdims=True)
    d_trace = per_group(d_trace) / trace
    d_cov = d_normed / trace + d_trace * eye
    both = d_cov + d_cov.T
    d_avg = -(dot_high(gf_row, whiten) + dot_high(avg, both))
    return whiten, offset_col, both / count, d_avg / count, column


def terms_kernel(count, place_ref, pay_ref, w_ref, left_ref, shift_ref, row_ref):
    stats = jnp.sum(pay_ref[...], axis=0)
    whiten, offset_col, symmetric, d_first, column = whiten_terms(stats, count)
    weight = w_ref[...].astype(F32)
    from_g = dot_high(weight, whiten, ((0,), (1,)))
    from_m = dot_high(weight, symmetric, ((0,), (0,)))
    bias_col = column(dot_high(d_first, weight))
    hidden_mat = jnp.concatenate([from_g, from_m], axis=1)
    full = jnp.concatenate(
        [hidden_mat, jnp.concatenate([jnp.zeros((C, C), F32), whiten], axis=1)], axis=0
    )
    coarse = full.astype(BF16)
    fine = (full - coarse.astype(F32)).astype(BF16)
    left_ref[...] = jnp.concatenate([coarse, fine], axis=1)
    shift_ref[0:C] = jnp.broadcast_to(bias_col, (C, W))
    shift_ref[C : 2 * C] = jnp.broadcast_to(-offset_col, (C, W))

    mine = place_ref[0]
    half = place_ref[3]
    pick = (iota((C, 1), 0) == mine).astype(F32)
    chosen = jnp.sum(pick * hidden_mat, axis=0, keepdims=True)
    chosen_bias = jnp.sum(pick * bias_col, axis=0, keepdims=True)
    lane8 = iota((8, W), 1)
    slot = iota((8, W), 0)
    prod = stats[0:8] * jnp.concatenate([chosen, chosen], axis=1)
    prod = jnp.where(slot < HALF, prod, 0.0)
    low = jnp.sum(jnp.where(lane8 < 64, prod, 0.0), axis=1, keepdims=True)
    high = jnp.sum(jnp.where(lane8 < 64, 0.0, prod), axis=1, keepdims=True)
    line = slot + HALF * half
    to_low = jnp.where(line < 9, C + 3 * line, C + 3 * (line - 9) + 2)
    to_low = jnp.where(line == 13, C + 26, to_low)
    to_high = jnp.where(line < 9, C + 3 * line + 1, C + 3 * (line - 5) + 2)
    to_high = jnp.where(line == 13, -1, to_high)
    taps_row = jnp.where(lane8 == to_low, low, 0.0) + jnp.where(lane8 == to_high, high, 0.0)
    taps_row = jnp.sum(taps_row, axis=0, keepdims=True)
    lane = iota((1, W), 1)
    counts = stats[HALF : HALF + 1]
    ones_row = jnp.where((lane >= 64) & (lane < 91), counts, 0.0)
    ones_row = chosen_bias * pltpu.roll(ones_row, W - 32, 1)
    hidden_sum = jnp.sum(jnp.where(lane == 91, counts, 0.0), axis=1, keepdims=True)
    pair = pltpu.roll(stats[6:7], 64, 1)[:, 0:64]
    point = dot_high(pair, jnp.concatenate([whiten, symmetric], axis=0)) + hidden_sum * d_first
    point = jnp.concatenate([point, jnp.zeros((1, W - C), F32)], axis=1)
    row = (taps_row + jnp.where(half == 1, point + ones_row, 0.0)) * (1.0 / math.sqrt(count))
    row_ref[...] = jnp.broadcast_to(row, (2 * C, W))


def grads_kernel(place_ref, left_ref, shift_ref, lo_ref, first_ref, inner_ref, last_ref, hi_ref,
                 dk_ref, white_ref, dvol_ref, coarse_ref, fine_ref, out_ref):
    zeros = jnp.zeros((D + 2, C, W), BF16)
    for ref in (coarse_ref, fine_ref):
        ref[:, :, 0:W] = zeros
        ref[:, :, PW - W : PW] = zeros
    inside_lo = place_ref[1].astype(F32)
    inside_hi = place_ref[2].astype(F32)
    left = left_ref[...]
    bias = shift_ref[0:C, 0:1]
    minus_offset = shift_ref[C : 2 * C, 0:1]
    planes = [lo_ref, first_ref, inner_ref.at[0], inner_ref.at[1], last_ref, hi_ref]
    for p in range(D + 2):
        cells = planes[p][...]
        both = dot(left, jnp.concatenate([cells, cells], axis=0))
        d_hidden = both[0:C] + bias
        if p == 0:
            d_hidden = d_hidden * inside_lo
        elif p > D:
            d_hidden = d_hidden * inside_hi
        else:
            white = (both[C : 2 * C] + minus_offset).astype(BF16)
            white_ref[:, p - 1] = white.reshape(C, H, W)
        terms = two_terms(d_hidden)
        coarse_ref[p, :, W : W + HW] = terms[0]
        fine_ref[p, :, W : W + HW] = terms[1]
    matrix, last_taps = tap_matrices(dk_ref, True)
    terms = two_terms(matrix)
    matrix = jnp.concatenate(terms, axis=0)
    for z in range(D):
        for start in range(0, HW, SPAN):
            coarse = offsets([coarse_ref.at[z + a] for a in range(3)], start, SPAN)
            fine = offsets([fine_ref.at[z + a] for a in range(3)], start, SPAN)
            both = dot(matrix, jnp.concatenate(coarse[:8], axis=0))
            rest = dot(terms[0], jnp.concatenate(fine[:8], axis=0))
            last = coarse[8].astype(F32) + fine[8].astype(F32)
            rows = stencil_rows(both[:96] + both[96:] + rest, last, last_taps)
            out_ref[:, start : start + SPAN] = rows.astype(BF16)
        dvol_ref[:, z] = out_ref[...].reshape(C, H, W)


def finish_kernel(rows_ref, point_ref, taps_ref):
    rows = rows_ref[pl.ds(0, C, stride=2), :] + rows_ref[pl.ds(1, C, stride=2), :]
    point_ref[...] = rows[:, 0:C].T
    taps_ref[...] = rows[:, C : C + 27]


def cost(us):
    return pl.CostEstimate(flops=int(us * 1e8), bytes_accessed=int(us * 1e6), transcendentals=0)


def whole_step(volumes, depth_kernel, point_weight, cotangent):
    x = volumes[0]
    g = cotangent[0]
    samples = lax.axis_size("sample")
    slabs = lax.axis_size("space")
    count = float(D * HW * samples * slabs)
    forward = [(i, i + 1) for i in range(slabs - 1)]
    backward = [(i + 1, i) for i in range(slabs - 1)]
    scratch = [pltpu.VMEM((2, C, HW), BF16), pltpu.VMEM((208, HW), BF16)]
    vmem = pl.BlockSpec(memory_space=pltpu.VMEM)
    smem = pl.BlockSpec(memory_space=pltpu.SMEM)
    shape = jax.ShapeDtypeStruct
    near = lambda array: pltpu.with_memory_space_constraint(array, pltpu.VMEM)

    near_plane, far_plane = pl.pallas_call(
        edges_kernel,
        in_specs=[pl.BlockSpec(memory_space=pl.ANY)],
        out_shape=(pltpu.VMEM((C, H, W), BF16), pltpu.VMEM((C, H, W), BF16)),
        scratch_shapes=[pltpu.SemaphoreType.DMA((2,))],
        name="edges",
    )(x)
    partners = [(i, i ^ 1) for i in range(slabs) if i ^ 1 < slabs]
    others = [(i, i + 1 if i % 2 else i - 1) for i in range(1, slabs) if i % 2 == 0 or i + 1 < slabs]
    near_plane = lax.ppermute(near_plane, "space", partners)
    far_plane = lax.ppermute(far_plane, "space", others)
    gm_inner, acc, own, edge = pl.pallas_call(
        inner_kernel,
        out_shape=(
            pltpu.VMEM((2, 2 * C, HW), BF16),
            pltpu.VMEM((368, 256), F32),
            pltpu.VMEM((D, C, PW), BF16),
            pltpu.VMEM((2, C, HW), BF16),
        ),
        scratch_shapes=scratch,
        cost_estimate=cost(6),
        name="inner",
    )(x, g, depth_kernel, point_weight)
    gm_first, gm_last, send = pl.pallas_call(
        outer_kernel,
        out_shape=(
            pltpu.VMEM((2 * C, HW), BF16),
            pltpu.VMEM((2 * C, HW), BF16),
            pltpu.VMEM((C * ROWS, W), F32),
        ),
        scratch_shapes=[pltpu.VMEM((368, 256), F32), pltpu.VMEM((2, C, PW), BF16)] + scratch,
        cost_estimate=cost(6),
        name="outer",
    )(
        near(own), near(edge), near(near_plane), near(far_plane), depth_kernel, point_weight,
        near(acc),
    )
    gm_lo = lax.ppermute(gm_last, "space", forward)
    gm_hi = lax.ppermute(gm_first, "space", backward)
    parts = lax.all_to_all(send.reshape(C, ROWS, W), "sample", 0, 0)
    part = pl.pallas_call(
        fold_kernel,
        in_specs=[vmem],
        out_shape=pltpu.VMEM((slabs, HALF + 9, W), F32),
        name="fold",
    )(near(parts))
    pay = lax.all_to_all(part, "space", 0, 0)
    slab = lax.axis_index("space")
    place = jnp.stack([
        lax.axis_index("sample"),
        (slab > 0).astype(jnp.int32),
        (slab < slabs - 1).astype(jnp.int32),
        slab % 2,
    ])
    left, shift, row = pl.pallas_call(
        lambda *refs: terms_kernel(count, *refs),
        in_specs=[smem] + [vmem] * 2,
        out_shape=(
            pltpu.VMEM((2 * C, 4 * C), BF16),
            pltpu.VMEM((2 * C, W), F32),
            pltpu.VMEM((2 * C, W), F32),
        ),
        cost_estimate=cost(4),
        name="terms",
    )(place, near(pay), point_weight)
    groups = [
        [sample * slabs + slab + i for sample in range(samples) for i in range(2)]
        for slab in range(0, slabs, 2)
    ]
    rows = lax.all_to_all(
        row.reshape(2 * C, 1, W), ("sample", "space"), 0, 0, axis_index_groups=groups
    ).reshape(2 * C, W)
    white, d_volume = pl.pallas_call(
        grads_kernel,
        in_specs=[smem] + [vmem] * 8,
        out_shape=(shape((C, D, H, W), BF16), shape((C, D, H, W), BF16)),
        scratch_shapes=[
            pltpu.VMEM((D + 2, C, PW), BF16),
            pltpu.VMEM((D + 2, C, PW), BF16),
            pltpu.VMEM((C, HW), BF16),
        ],
        cost_estimate=cost(8),
        name="grads",
    )(
        place, near(left), near(shift), near(gm_lo), near(gm_first), near(gm_inner),
        near(gm_last), near(gm_hi), depth_kernel,
    )
    d_point, d_kernel = pl.pallas_call(
        finish_kernel,
        out_shape=(shape((C, C), F32), shape((C, 27), F32)),
        in_specs=[vmem],
        name="finish",
    )(near(rows))
    return white[None], d_volume[None], d_point, d_kernel


def solution(mesh):
    split = P("sample", None, "space", None, None)
    return jax.shard_map(
        whole_step,
        mesh=mesh,
        in_specs=(split, P(), P(), split),
        out_specs=(split, split, P(), P()),
        check_vma=False,
    )
```

```python
import math

import jax
import jax.numpy as jnp
from jax import lax
from jax.experimental import pallas as pl
from jax.experimental.pallas import tpu as pltpu
from jax.sharding import PartitionSpec as P


NEWTON = 5
EPSILON = 1e-05
C = 32
D = 4
H = 16
W = 128
HW = H * W
PW = (H + 2) * W
SPAN = 512
ROWS = 24
HIGH = lax.Precision.HIGHEST
F32 = jnp.float32
BF16 = jnp.bfloat16


def dot(a, b, dims=((1,), (0,)), precision=None):
    return lax.dot_general(
        a, b, (dims, ((), ())), precision=precision, preferred_element_type=F32
    )


def dot_high(a, b, dims=((1,), (0,))):
    return dot(a, b, dims, HIGH)


def iota(shape, dim):
    return lax.broadcasted_iota(jnp.int32, shape, dim)


def two_terms(values):
    coarse = values.astype(BF16)
    return coarse, (values - coarse.astype(F32)).astype(BF16)


def tap_matrices(dk_ref, flip):
    row = iota((C, W), 0)
    lane = iota((C, W), 1)
    taps = [
        jnp.broadcast_to(dk_ref[:, (26 - t if flip else t) : (27 - t if flip else t + 1)], (C, W))
        for t in range(27)
    ]
    blocks = []
    for e in range(3):
        halves = []
        for half in range(2):
            block = jnp.zeros((C, W), F32)
            for i in range(4):
                block = jnp.where(lane == row + C * i, taps[3 * (4 * half + i) + e], block)
            halves.append(block)
        blocks.append(jnp.concatenate(halves, axis=1))
    return jnp.concatenate(blocks, axis=0), taps[24:27]


def stencil_rows(sums, last, last_taps):
    lane = iota((C, W), 1)
    rows = []
    for i in range(last.shape[1] // W):
        span = slice(i * W, (i + 1) * W)
        parts = [sums[C * e : C * (e + 1), span] + last_taps[e] * last[:, span] for e in range(3)]
        left = jnp.where(lane == 0, 0.0, pltpu.roll(parts[0], 1, 1))
        right = jnp.where(lane == W - 1, 0.0, pltpu.roll(parts[2], W - 1, 1))
        rows.append(parts[1] + left + right)
    return jnp.concatenate(rows, axis=1)


def offsets(planes, start, width):
    return [
        planes[a][:, start + b * W : start + b * W + width] for a in range(3) for b in range(3)
    ]


def fill_plane(ref, cells):
    zeros = jnp.zeros((C, W), BF16)
    ref[:, 0:W] = zeros
    ref[:, PW - W : PW] = zeros
    ref[:, W : W + HW] = cells.reshape(C, HW)


def slab_sums(triples, gs, dk_ref, w_ref, gm_refs, acc_ref, hid_ref, right_ref):
    matrix, last_taps = tap_matrices(dk_ref, False)
    matrix = jnp.concatenate(two_terms(matrix), axis=0)
    for i in range(len(triples)):
        for start in range(0, HW, SPAN):
            cells = offsets(triples[i], start, SPAN)
            both = dot(matrix, jnp.concatenate(cells[:8], axis=0))
            rows = stencil_rows(both[:96] + both[96:], cells[8].astype(F32), last_taps)
            hid_ref[i, :, start : start + SPAN] = rows.astype(BF16)

    lane = iota((1, W), 1)
    row16 = iota((16, W), 0)
    lane16 = iota((16, W), 1)
    keep0 = (lane < W - 1).astype(F32).astype(BF16)
    keep2 = (lane > 0).astype(F32).astype(BF16)
    ones = jnp.where(
        ((row16 == 0) & (lane16 < W - 1)) | (row16 == 1) | ((row16 == 2) & (lane16 > 0)),
        1.0, 0.0,
    ).astype(BF16)
    for h in range(H):
        right_ref[192:208, h * W : (h + 1) * W] = ones
    first = jnp.where(iota((16, HW), 0) == 0, 1.0, 0.0).astype(BF16)
    for i in range(len(triples)):
        hidden = hid_ref[i]
        mixed = dot(w_ref[...], hidden).astype(BF16)
        gm_refs[i][0:C, :] = gs[i]()
        gm_refs[i][C : 2 * C, :] = mixed
        for h in range(H):
            span = slice(h * W, (h + 1) * W)
            cells = gm_refs[i][:, span]
            right_ref[0:64, span] = pltpu.roll(cells, W - 1, 1) * keep0
            right_ref[64:128, span] = cells
            right_ref[128:192, span] = pltpu.roll(cells, 1, 1) * keep2
        left = offsets(triples[i], 0, HW) + [hidden, mixed, first]
        acc_ref[:, 0:208] += dot(
            jnp.concatenate(left, axis=0), right_ref[...], ((1,), (1,))
        )


def edges_kernel(x_ref, near_ref, far_ref, sems):
    even = lax.rem(lax.axis_index("space"), 2) == 0
    plane = jnp.where(even, D - 1, 0)
    first = pltpu.make_async_copy(x_ref.at[:, plane], near_ref, sems.at[0])
    last = pltpu.make_async_copy(x_ref.at[:, D - 1 - plane], far_ref, sems.at[1])
    first.start()
    last.start()
    first.wait()
    last.wait()


def inner_kernel(x_ref, g_ref, dk_ref, w_ref, gm_ref, acc_ref, own_ref, edge_ref, *scratch):
    acc_ref[...] = jnp.zeros(acc_ref.shape, F32)
    for p in range(D):
        fill_plane(own_ref.at[p], x_ref[:, p])
    for i, p in enumerate((0, D - 1)):
        edge_ref[i] = g_ref[:, p].reshape(C, HW)
    triples = [[own_ref.at[i + a] for a in range(3)] for i in range(2)]
    gs = [lambda p=p: g_ref[:, p].reshape(C, HW) for p in (1, 2)]
    slab_sums(triples, gs, dk_ref, w_ref, (gm_ref.at[0], gm_ref.at[1]), acc_ref, *scratch)


def outer_sums(on_partner, own_ref, edge_ref, halo_ref, dk_ref, w_ref, part_ref,
               gm_ref, acc_ref, planes_ref, *scratch):
    acc_ref[...] = part_ref[...]
    even = lax.rem(lax.axis_index("space"), 2)
    even = 1 - even if on_partner else even
    top = even == 1
    source = jnp.where(top, D - 2, 0)
    target = jnp.where(top, 0, 1)
    for i in range(2):
        planes_ref[target + i] = own_ref[source + i]
    fill_plane(planes_ref.at[jnp.where(top, 2, 0)], halo_ref[...])
    triple = [planes_ref.at[a] for a in range(3)]
    gs = [lambda: edge_ref[jnp.where(top, 1, 0)]]
    slab_sums([triple], gs, dk_ref, w_ref, (gm_ref,), acc_ref, *scratch)


def near_kernel(*refs):
    outer_sums(True, *refs)


def far_kernel(own_ref, edge_ref, halo_ref, dk_ref, w_ref, part_ref, gm_ref, send_ref, acc_ref,
               *scratch):
    outer_sums(
        False, own_ref, edge_ref, halo_ref, dk_ref, w_ref, part_ref, gm_ref, acc_ref, *scratch
    )

    def put(row, slab):
        send_ref[pl.ds(row, C, stride=ROWS), :] = slab

    lane = iota((C, W), 1)
    tile1 = [acc_ref[C * i : C * (i + 1), 128:256] for i in range(10)]
    for ab in range(9):
        put(ab, acc_ref[C * ab : C * (ab + 1), 0:128])
    for i in range(4):
        put(9 + i, jnp.where(lane < 64, tile1[i], pltpu.roll(tile1[4 + i], 64, 1)))
    put(13, jnp.where(lane < 64, tile1[8], acc_ref[288:320, 0:128]))
    counts = jnp.broadcast_to(pltpu.roll(acc_ref[352:353, 0:128], 64, 1), (C, W))
    counts = jnp.where(lane < 64, counts, 0.0)
    for ab in range(9):
        own = jnp.where((lane >= 64) & (lane < 67), tile1[ab], 0.0)
        counts = counts + pltpu.roll(own, 3 * ab, 1)
    counts = counts + pltpu.roll(jnp.where(lane == 65, tile1[9], 0.0), 26, 1)
    put(14, counts)
    put(15, jnp.zeros((C, W), F32))
    row = iota((C, W), 0)
    stats = pltpu.roll(acc_ref[320:352, 0:128], 64, 1)
    second = pltpu.roll(stats, 96, 1)
    swapped = jnp.where(lane < 16, pltpu.roll(stats, 112, 1), pltpu.roll(stats, 16, 1))
    mine = (row < 16) == (lane < 16)
    table = jnp.where(lane < C, jnp.where(mine, second, swapped), 0.0)
    packed = table[0:8]
    for q in range(1, 4):
        packed = packed + pltpu.roll(table[8 * q : 8 * q + 8], 32 * q, 1)
    for r in range(8):
        put(16 + r, jnp.broadcast_to(packed[r : r + 1], (C, W)))


def whiten_terms(stats, count):
    gf_row = stats[14:15, 0:C]
    first_row = stats[14:15, C : 2 * C]
    packed = stats[16:24]
    table = jnp.concatenate([pltpu.roll(packed, (W - 32 * q) % W, 1) for q in range(4)], axis=0)
    table = table[:, 0:C]
    row = iota((C, C), 0)
    col = iota((C, C), 1)
    mine = (row < 16) == (col < 16)
    eye = (row == col).astype(F32)
    low = iota((1, C), 1) < 16
    second = jnp.where(mine, table, 0.0)
    other = jnp.concatenate([table[:, 16:32], table[:, 0:16]], axis=1)
    grad_mat = jnp.where(mine, other, 0.0).T

    def column(values):
        return jnp.sum(eye * values, axis=1, keepdims=True)

    def per_group(values):
        left = jnp.sum(jnp.where(low, values, 0.0), axis=1, keepdims=True)
        right = jnp.sum(jnp.where(low, 0.0, values), axis=1, keepdims=True)
        return jnp.where(low, left, right)

    avg = first_row / count
    avg_col = column(avg)
    cov = second / count - jnp.where(mine, avg_col * avg, 0.0) + EPSILON * eye
    trace = per_group(jnp.sum(cov * eye, axis=0, keepdims=True))
    normed = cov / trace
    d_whiten = grad_mat - jnp.where(mine, column(gf_row) * avg, 0.0)

    project = 1.5 * eye - 0.5 * normed
    slope = -0.5 * d_whiten
    for _ in range(NEWTON - 1):
        pair = jnp.concatenate([project, slope], axis=0)
        squares = dot_high(pair, project)
        scaled = dot_high(pair, normed)
        square = squares[0:C]
        d_square = squares[C : 2 * C] + dot_high(project, slope)
        d_scaled = scaled[C : 2 * C] + dot_high(project, d_whiten)
        cubes = dot_high(jnp.concatenate([square, d_square], axis=0), scaled[0:C])
        slope = 1.5 * slope - 0.5 * (cubes[C : 2 * C] + dot_high(square, d_scaled))
        project = 1.5 * project - 0.5 * cubes[0:C]
    root = jnp.sqrt(trace)
    whiten = project / root
    offset_col = jnp.sum(whiten * avg, axis=1, keepdims=True)
    d_normed = slope / root
    d_trace = jnp.sum(-0.5 * d_whiten * whiten - d_normed * normed, axis=0, keepdims=True)
    d_trace = per_group(d_trace) / trace
    d_cov = d_normed / trace + d_trace * eye
    both = d_cov + d_cov.T
    d_avg = -(dot_high(gf_row, whiten) + dot_high(avg, both))
    return whiten, offset_col, both / count, d_avg / count, column


def terms_kernel(count, place_ref, pay_ref, w_ref, left_ref, shift_ref, row_ref):
    stats = jnp.sum(pay_ref[...], axis=0)
    whiten, offset_col, symmetric, d_first, column = whiten_terms(stats, count)
    weight = w_ref[...].astype(F32)
    from_g = dot_high(weight, whiten, ((0,), (1,)))
    from_m = dot_high(weight, symmetric, ((0,), (0,)))
    bias_col = column(dot_high(d_first, weight))
    hidden_mat = jnp.concatenate([from_g, from_m], axis=1)
    full = jnp.concatenate(
        [hidden_mat, jnp.concatenate([jnp.zeros((C, C), F32), whiten], axis=1)], axis=0
    )
    coarse = full.astype(BF16)
    fine = (full - coarse.astype(F32)).astype(BF16)
    left_ref[...] = jnp.concatenate([coarse, fine], axis=1)
    shift_ref[0:C] = jnp.broadcast_to(bias_col, (C, W))
    shift_ref[C : 2 * C] = jnp.broadcast_to(-offset_col, (C, W))

    mine = place_ref[0]
    pick = (iota((C, 1), 0) == mine).astype(F32)
    chosen = jnp.sum(pick * hidden_mat, axis=0, keepdims=True)
    chosen_bias = jnp.sum(pick * bias_col, axis=0, keepdims=True)
    prod = stats[0:16] * jnp.concatenate([chosen, chosen], axis=1)
    lane16 = iota((16, W), 1)
    row16 = iota((16, W), 0)
    low = jnp.sum(jnp.where(lane16 < 64, prod, 0.0), axis=1, keepdims=True)
    high = jnp.sum(jnp.where(lane16 < 64, 0.0, prod), axis=1, keepdims=True)
    to_low = jnp.where(row16 < 9, C + 3 * row16, C + 3 * (row16 - 9) + 2)
    to_low = jnp.where(row16 == 13, C + 26, jnp.where(row16 > 13, -1, to_low))
    to_high = jnp.where(row16 < 9, C + 3 * row16 + 1, C + 3 * (row16 - 5) + 2)
    to_high = jnp.where(row16 > 12, -1, to_high)
    taps_row = jnp.where(lane16 == to_low, low, 0.0) + jnp.where(lane16 == to_high, high, 0.0)
    taps_row = jnp.sum(taps_row, axis=0, keepdims=True)
    lane = iota((1, W), 1)
    ones_row = jnp.where((lane >= 64) & (lane < 91), stats[14:15], 0.0)
    taps_row = taps_row + chosen_bias * pltpu.roll(ones_row, W - 32, 1)
    hidden_sum = jnp.sum(jnp.where(lane == 91, stats[14:15], 0.0), axis=1, keepdims=True)
    pair = pltpu.roll(stats[13:14], 64, 1)[:, 0:64]
    point = dot_high(pair, jnp.concatenate([whiten, symmetric], axis=0)) + hidden_sum * d_first
    point = jnp.concatenate([point, jnp.zeros((1, W - C), F32)], axis=1)
    row = (taps_row + point) * (1.0 / math.sqrt(count))
    row_ref[...] = jnp.broadcast_to(row, (C, W))


def grads_kernel(place_ref, left_ref, shift_ref, near_in_ref, near_ref, inner_ref, far_ref, far_in_ref,
                 dk_ref, white_ref, dvol_ref, coarse_ref, fine_ref, out_ref):
    zeros = jnp.zeros((D + 2, C, W), BF16)
    for ref in (coarse_ref, fine_ref):
        ref[:, :, 0:W] = zeros
        ref[:, :, PW - W : PW] = zeros
    inside_lo = place_ref[1].astype(F32)
    inside_hi = place_ref[2].astype(F32)
    left = left_ref[...]
    bias = shift_ref[0:C, 0:1]
    minus_offset = shift_ref[C : 2 * C, 0:1]
    even = lax.rem(lax.axis_index("space"), 2) == 0
    planes = [
        lambda: jnp.where(even, far_in_ref[...], near_in_ref[...]),
        lambda: jnp.where(even, far_ref[...], near_ref[...]),
        lambda: inner_ref[0],
        lambda: inner_ref[1],
        lambda: jnp.where(even, near_ref[...], far_ref[...]),
        lambda: jnp.where(even, near_in_ref[...], far_in_ref[...]),
    ]
    for p in range(D + 2):
        cells = planes[p]()
        both = dot(left, jnp.concatenate([cells, cells], axis=0))
        d_hidden = both[0:C] + bias
        if p == 0:
            d_hidden = d_hidden * inside_lo
        elif p > D:
            d_hidden = d_hidden * inside_hi
        else:
            white = (both[C : 2 * C] + minus_offset).astype(BF16)
            white_ref[:, p - 1] = white.reshape(C, H, W)
        terms = two_terms(d_hidden)
        coarse_ref[p, :, W : W + HW] = terms[0]
        fine_ref[p, :, W : W + HW] = terms[1]
    matrix, last_taps = tap_matrices(dk_ref, True)
    terms = two_terms(matrix)
    matrix = jnp.concatenate(terms, axis=0)
    for z in range(D):
        for start in range(0, HW, SPAN):
            coarse = offsets([coarse_ref.at[z + a] for a in range(3)], start, SPAN)
            fine = offsets([fine_ref.at[z + a] for a in range(3)], start, SPAN)
            both = dot(matrix, jnp.concatenate(coarse[:8], axis=0))
            rest = dot(terms[0], jnp.concatenate(fine[:8], axis=0))
            last = coarse[8].astype(F32) + fine[8].astype(F32)
            rows = stencil_rows(both[:96] + both[96:] + rest, last, last_taps)
            out_ref[:, start : start + SPAN] = rows.astype(BF16)
        dvol_ref[:, z] = out_ref[...].reshape(C, H, W)


def finish_kernel(rows_ref, point_ref, taps_ref):
    rows = rows_ref[...]
    point_ref[...] = rows[:, 0:C].T
    taps_ref[...] = rows[:, C : C + 27]


def cost(us):
    return pl.CostEstimate(flops=int(us * 1e8), bytes_accessed=int(us * 1e6), transcendentals=0)


def whole_step(volumes, depth_kernel, point_weight, cotangent):
    x = volumes[0]
    g = cotangent[0]
    samples = lax.axis_size("sample")
    slabs = lax.axis_size("space")
    count = float(D * HW * samples * slabs)
    scratch = [pltpu.VMEM((2, C, HW), BF16), pltpu.VMEM((208, HW), BF16)]
    vmem = pl.BlockSpec(memory_space=pltpu.VMEM)
    smem = pl.BlockSpec(memory_space=pltpu.SMEM)
    shape = jax.ShapeDtypeStruct
    near = lambda array: pltpu.with_memory_space_constraint(array, pltpu.VMEM)

    near_plane, far_plane = pl.pallas_call(
        edges_kernel,
        in_specs=[pl.BlockSpec(memory_space=pl.ANY)],
        out_shape=(pltpu.VMEM((C, H, W), BF16), pltpu.VMEM((C, H, W), BF16)),
        scratch_shapes=[pltpu.SemaphoreType.DMA((2,))],
        name="edges",
    )(x)
    partners = [(i, i ^ 1) for i in range(slabs) if i ^ 1 < slabs]
    others = [(i, i + 1 if i % 2 else i - 1) for i in range(1, slabs) if i % 2 == 0 or i + 1 < slabs]
    near_plane = lax.ppermute(near_plane, "space", partners)
    far_plane = lax.ppermute(far_plane, "space", others)
    gm_inner, acc, own, edge = pl.pallas_call(
        inner_kernel,
        out_shape=(
            pltpu.VMEM((2, 2 * C, HW), BF16),
            pltpu.VMEM((368, 256), F32),
            pltpu.VMEM((D, C, PW), BF16),
            pltpu.VMEM((2, C, HW), BF16),
        ),
        scratch_shapes=scratch,
        cost_estimate=cost(6),
        name="inner",
    )(x, g, depth_kernel, point_weight)
    scratch = [pltpu.VMEM((3, C, PW), BF16), pltpu.VMEM((1, C, HW), BF16), scratch[1]]
    gm_near, acc = pl.pallas_call(
        near_kernel,
        out_shape=(pltpu.VMEM((2 * C, HW), BF16), pltpu.VMEM((368, 256), F32)),
        scratch_shapes=scratch,
        cost_estimate=cost(3),
        compiler_params=pltpu.CompilerParams(vmem_limit_bytes=48 << 20),
        name="near",
    )(near(own), near(edge), near(near_plane), depth_kernel, point_weight, near(acc))
    gm_far, send = pl.pallas_call(
        far_kernel,
        out_shape=(pltpu.VMEM((2 * C, HW), BF16), pltpu.VMEM((C * ROWS, W), F32)),
        scratch_shapes=[pltpu.VMEM((368, 256), F32)] + scratch,
        cost_estimate=cost(3),
        compiler_params=pltpu.CompilerParams(vmem_limit_bytes=48 << 20),
        name="far",
    )(near(own), near(edge), near(far_plane), depth_kernel, point_weight, near(acc))
    near_in = lax.ppermute(gm_near, "space", partners)
    far_in = lax.ppermute(gm_far, "space", others)
    parts = lax.all_to_all(send.reshape(C, ROWS, W), "sample", 0, 0)
    part = jnp.broadcast_to(jnp.sum(parts, axis=0), (slabs, ROWS, W))
    pay = lax.all_to_all(part, "space", 0, 0)
    slab = lax.axis_index("space")
    place = jnp.stack([
        lax.axis_index("sample"),
        (slab > 0).astype(jnp.int32),
        (slab < slabs - 1).astype(jnp.int32),
    ])
    left, shift, row = pl.pallas_call(
        lambda *refs: terms_kernel(count, *refs),
        in_specs=[smem] + [vmem] * 2,
        out_shape=(
            pltpu.VMEM((2 * C, 4 * C), BF16),
            pltpu.VMEM((2 * C, W), F32),
            pltpu.VMEM((C, W), F32),
        ),
        cost_estimate=cost(4),
        name="terms",
    )(place, near(pay), point_weight)
    rows = lax.all_to_all(row.reshape(C, 1, W), "sample", 0, 0).reshape(C, W)
    white, d_volume = pl.pallas_call(
        grads_kernel,
        in_specs=[smem] + [vmem] * 8,
        out_shape=(shape((C, D, H, W), BF16), shape((C, D, H, W), BF16)),
        scratch_shapes=[
            pltpu.VMEM((D + 2, C, PW), BF16),
            pltpu.VMEM((D + 2, C, PW), BF16),
            pltpu.VMEM((C, HW), BF16),
        ],
        cost_estimate=cost(8),
        name="grads",
    )(
        place, near(left), near(shift), near(near_in), near(gm_near), near(gm_inner),
        near(gm_far), near(far_in), depth_kernel,
    )
    d_point, d_kernel = pl.pallas_call(
        finish_kernel,
        out_shape=(shape((C, C), F32), shape((C, 27), F32)),
        in_specs=[vmem],
        name="finish",
    )(near(rows))
    return white[None], d_volume[None], d_point, d_kernel


def solution(mesh):
    split = P("sample", None, "space", None, None)
    return jax.shard_map(
        whole_step,
        mesh=mesh,
        in_specs=(split, P(), P(), split),
        out_specs=(split, split, P(), P()),
        check_vma=False,
    )
```

```python
import math

import jax
import jax.numpy as jnp
from jax import lax
from jax.experimental import pallas as pl
from jax.experimental.pallas import tpu as pltpu
from jax.sharding import PartitionSpec as P


NEWTON = 5
EPSILON = 1e-05
C = 32
D = 4
H = 16
W = 128
HW = H * W
PW = (H + 2) * W
SPAN = 512
ROWS = 24
HIGH = lax.Precision.HIGHEST
F32 = jnp.float32
BF16 = jnp.bfloat16


def dot(a, b, dims=((1,), (0,)), precision=None):
    return lax.dot_general(
        a, b, (dims, ((), ())), precision=precision, preferred_element_type=F32
    )


def dot_high(a, b, dims=((1,), (0,))):
    return dot(a, b, dims, HIGH)


def iota(shape, dim):
    return lax.broadcasted_iota(jnp.int32, shape, dim)


def two_terms(values):
    coarse = values.astype(BF16)
    return coarse, (values - coarse.astype(F32)).astype(BF16)


def tap_matrices(dk_ref, flip):
    row = iota((C, W), 0)
    lane = iota((C, W), 1)
    taps = [
        jnp.broadcast_to(dk_ref[:, (26 - t if flip else t) : (27 - t if flip else t + 1)], (C, W))
        for t in range(27)
    ]
    blocks = []
    for e in range(3):
        halves = []
        for half in range(2):
            block = jnp.zeros((C, W), F32)
            for i in range(4):
                block = jnp.where(lane == row + C * i, taps[3 * (4 * half + i) + e], block)
            halves.append(block)
        blocks.append(jnp.concatenate(halves, axis=1))
    return jnp.concatenate(blocks, axis=0), taps[24:27]


def stencil_rows(sums, last, last_taps):
    lane = iota((C, W), 1)
    rows = []
    for i in range(last.shape[1] // W):
        span = slice(i * W, (i + 1) * W)
        parts = [sums[C * e : C * (e + 1), span] + last_taps[e] * last[:, span] for e in range(3)]
        left = jnp.where(lane == 0, 0.0, pltpu.roll(parts[0], 1, 1))
        right = jnp.where(lane == W - 1, 0.0, pltpu.roll(parts[2], W - 1, 1))
        rows.append(parts[1] + left + right)
    return jnp.concatenate(rows, axis=1)


def offsets(planes, start, width):
    return [
        planes[a][:, start + b * W : start + b * W + width] for a in range(3) for b in range(3)
    ]


def fill_plane(ref, cells):
    zeros = jnp.zeros((C, W), BF16)
    ref[:, 0:W] = zeros
    ref[:, PW - W : PW] = zeros
    ref[:, W : W + HW] = cells.reshape(C, HW)


def slab_sums(triples, gs, matrix, last_taps, w_ref, gm_refs, base, acc_ref, hid_ref, right_ref):
    for i in range(len(triples)):
        for start in range(0, HW, SPAN):
            cells = offsets(triples[i], start, SPAN)
            both = dot(matrix, jnp.concatenate(cells[:8], axis=0))
            rows = stencil_rows(both[:96] + both[96:], cells[8].astype(F32), last_taps)
            hid_ref[i, :, start : start + SPAN] = rows.astype(BF16)

    lane = iota((1, W), 1)
    row16 = iota((16, W), 0)
    lane16 = iota((16, W), 1)
    keep0 = (lane < W - 1).astype(F32).astype(BF16)
    keep2 = (lane > 0).astype(F32).astype(BF16)
    ones = jnp.where(
        ((row16 == 0) & (lane16 < W - 1)) | (row16 == 1) | ((row16 == 2) & (lane16 > 0)),
        1.0, 0.0,
    ).astype(BF16)
    for h in range(H):
        right_ref[192:208, h * W : (h + 1) * W] = ones
    first = jnp.where(iota((16, HW), 0) == 0, 1.0, 0.0).astype(BF16)
    for i in range(len(triples)):
        hidden = hid_ref[i]
        mixed = dot(w_ref[...], hidden).astype(BF16)
        gm_refs[i][0:C, :] = gs[i]()
        gm_refs[i][C : 2 * C, :] = mixed
        for h in range(H):
            span = slice(h * W, (h + 1) * W)
            cells = gm_refs[i][:, span]
            right_ref[0:64, span] = pltpu.roll(cells, W - 1, 1) * keep0
            right_ref[64:128, span] = cells
            right_ref[128:192, span] = pltpu.roll(cells, 1, 1) * keep2
        left = offsets(triples[i], 0, HW) + [hidden, mixed, first]
        product = dot(jnp.concatenate(left, axis=0), right_ref[...], ((1,), (1,)))
        acc_ref[:, 0:208] = product if base is None else base[:, 0:208] + product
        base = acc_ref


def edges_kernel(x_ref, near_ref, far_ref, sems):
    even = lax.rem(lax.axis_index("space"), 2) == 0
    plane = jnp.where(even, D - 1, 0)
    copies = []
    for i in range(4):
        part = pl.ds(8 * i, 8)
        for side, (ref, p) in enumerate(((near_ref, plane), (far_ref, D - 1 - plane))):
            copies.append(
                pltpu.make_async_copy(x_ref.at[part, p], ref.at[part], sems.at[2 * i + side])
            )
    for copy in copies:
        copy.start()
    for copy in copies:
        copy.wait()


def inner_kernel(x_ref, g_ref, dk_ref, w_ref, gm_ref, acc_ref, own_ref, edge_ref, matrix_ref,
                 last_ref, *scratch):
    matrix, last_taps = tap_matrices(dk_ref, False)
    matrix_ref[...] = jnp.concatenate(two_terms(matrix), axis=0)
    for e in range(3):
        last_ref[e] = last_taps[e]
    for p in range(D):
        fill_plane(own_ref.at[p], x_ref[:, p])
    for i, p in enumerate((0, D - 1)):
        edge_ref[i] = g_ref[:, p].reshape(C, HW)
    triples = [[own_ref.at[i + a] for a in range(3)] for i in range(2)]
    gs = [lambda p=p: g_ref[:, p].reshape(C, HW) for p in (1, 2)]
    gm_refs = (gm_ref.at[0], gm_ref.at[1])
    slab_sums(triples, gs, matrix_ref[...], last_taps, w_ref, gm_refs, None, acc_ref, *scratch)


def outer_sums(on_partner, own_ref, edge_ref, halo_ref, matrix_ref, last_ref, w_ref, part_ref,
               gm_ref, acc_ref, planes_ref, *scratch):
    even = lax.rem(lax.axis_index("space"), 2)
    even = 1 - even if on_partner else even
    top = even == 1
    source = jnp.where(top, D - 2, 0)
    target = jnp.where(top, 0, 1)
    for i in range(2):
        planes_ref[target + i] = own_ref[source + i]
    fill_plane(planes_ref.at[jnp.where(top, 2, 0)], halo_ref[...])
    triple = [planes_ref.at[a] for a in range(3)]
    gs = [lambda: edge_ref[jnp.where(top, 1, 0)]]
    last_taps = [last_ref[e] for e in range(3)]
    slab_sums(
        [triple], gs, matrix_ref[...], last_taps, w_ref, (gm_ref,), part_ref, acc_ref, *scratch
    )


def near_kernel(*refs):
    outer_sums(True, *refs)


def far_kernel(own_ref, edge_ref, halo_ref, matrix_ref, last_ref, w_ref, part_ref, gm_ref,
               send_ref, acc_ref, *scratch):
    outer_sums(
        False, own_ref, edge_ref, halo_ref, matrix_ref, last_ref, w_ref, part_ref, gm_ref,
        acc_ref, *scratch,
    )

    def put(row, slab):
        send_ref[pl.ds(row, C, stride=ROWS), :] = slab

    lane = iota((C, W), 1)
    tile1 = [acc_ref[C * i : C * (i + 1), 128:256] for i in range(10)]
    for ab in range(9):
        put(ab, acc_ref[C * ab : C * (ab + 1), 0:128])
    for i in range(4):
        put(9 + i, jnp.where(lane < 64, tile1[i], pltpu.roll(tile1[4 + i], 64, 1)))
    put(13, jnp.where(lane < 64, tile1[8], acc_ref[288:320, 0:128]))
    counts = jnp.broadcast_to(pltpu.roll(acc_ref[352:353, 0:128], 64, 1), (C, W))
    counts = jnp.where(lane < 64, counts, 0.0)
    for ab in range(9):
        own = jnp.where((lane >= 64) & (lane < 67), tile1[ab], 0.0)
        counts = counts + pltpu.roll(own, 3 * ab, 1)
    counts = counts + pltpu.roll(jnp.where(lane == 65, tile1[9], 0.0), 26, 1)
    put(14, counts)
    put(15, jnp.zeros((C, W), F32))
    row = iota((C, W), 0)
    stats = pltpu.roll(acc_ref[320:352, 0:128], 64, 1)
    second = pltpu.roll(stats, 96, 1)
    swapped = jnp.where(lane < 16, pltpu.roll(stats, 112, 1), pltpu.roll(stats, 16, 1))
    mine = (row < 16) == (lane < 16)
    table = jnp.where(lane < C, jnp.where(mine, second, swapped), 0.0)
    packed = table[0:8]
    for q in range(1, 4):
        packed = packed + pltpu.roll(table[8 * q : 8 * q + 8], 32 * q, 1)
    for r in range(8):
        put(16 + r, jnp.broadcast_to(packed[r : r + 1], (C, W)))


def whiten_terms(stats, count):
    gf_row = stats[14:15, 0:C]
    first_row = stats[14:15, C : 2 * C]
    packed = stats[16:24]
    table = jnp.concatenate([pltpu.roll(packed, (W - 32 * q) % W, 1) for q in range(4)], axis=0)
    table = table[:, 0:C]
    row = iota((C, C), 0)
    col = iota((C, C), 1)
    mine = (row < 16) == (col < 16)
    eye = (row == col).astype(F32)
    low = iota((1, C), 1) < 16
    second = jnp.where(mine, table, 0.0)
    other = jnp.concatenate([table[:, 16:32], table[:, 0:16]], axis=1)
    grad_mat = jnp.where(mine, other, 0.0).T

    def column(values):
        return jnp.sum(eye * values, axis=1, keepdims=True)

    def per_group(values):
        left = jnp.sum(jnp.where(low, values, 0.0), axis=1, keepdims=True)
        right = jnp.sum(jnp.where(low, 0.0, values), axis=1, keepdims=True)
        return jnp.where(low, left, right)

    avg = first_row / count
    avg_col = column(avg)
    cov = second / count - jnp.where(mine, avg_col * avg, 0.0) + EPSILON * eye
    trace = per_group(jnp.sum(cov * eye, axis=0, keepdims=True))
    normed = cov / trace
    d_whiten = grad_mat - jnp.where(mine, column(gf_row) * avg, 0.0)

    project = 1.5 * eye - 0.5 * normed
    slope = -0.5 * d_whiten
    for _ in range(NEWTON - 1):
        pair = jnp.concatenate([project, slope], axis=0)
        squares = dot_high(pair, project)
        scaled = dot_high(pair, normed)
        square = squares[0:C]
        d_square = squares[C : 2 * C] + dot_high(project, slope)
        d_scaled = scaled[C : 2 * C] + dot_high(project, d_whiten)
        cubes = dot_high(jnp.concatenate([square, d_square], axis=0), scaled[0:C])
        slope = 1.5 * slope - 0.5 * (cubes[C : 2 * C] + dot_high(square, d_scaled))
        project = 1.5 * project - 0.5 * cubes[0:C]
    root = jnp.sqrt(trace)
    whiten = project / root
    offset_col = jnp.sum(whiten * avg, axis=1, keepdims=True)
    d_normed = slope / root
    d_trace = jnp.sum(-0.5 * d_whiten * whiten - d_normed * normed, axis=0, keepdims=True)
    d_trace = per_group(d_trace) / trace
    d_cov = d_normed / trace + d_trace * eye
    both = d_cov + d_cov.T
    d_avg = -(dot_high(gf_row, whiten) + dot_high(avg, both))
    return whiten, offset_col, both / count, d_avg / count, column


def terms_kernel(count, place_ref, pay_ref, w_ref, left_ref, shift_ref, row_ref):
    stats = jnp.sum(pay_ref[...], axis=0)
    whiten, offset_col, symmetric, d_first, column = whiten_terms(stats, count)
    weight = w_ref[...].astype(F32)
    from_g = dot_high(weight, whiten, ((0,), (1,)))
    from_m = dot_high(weight, symmetric, ((0,), (0,)))
    bias_col = column(dot_high(d_first, weight))
    hidden_mat = jnp.concatenate([from_g, from_m], axis=1)
    full = jnp.concatenate(
        [hidden_mat, jnp.concatenate([jnp.zeros((C, C), F32), whiten], axis=1)], axis=0
    )
    coarse = full.astype(BF16)
    fine = (full - coarse.astype(F32)).astype(BF16)
    left_ref[...] = jnp.concatenate([coarse, fine], axis=1)
    shift_ref[0:C] = jnp.broadcast_to(bias_col, (C, W))
    shift_ref[C : 2 * C] = jnp.broadcast_to(-offset_col, (C, W))

    mine = place_ref[0]
    pick = (iota((C, 1), 0) == mine).astype(F32)
    chosen = jnp.sum(pick * hidden_mat, axis=0, keepdims=True)
    chosen_bias = jnp.sum(pick * bias_col, axis=0, keepdims=True)
    prod = stats[0:16] * jnp.concatenate([chosen, chosen], axis=1)
    lane16 = iota((16, W), 1)
    row16 = iota((16, W), 0)
    low = jnp.sum(jnp.where(lane16 < 64, prod, 0.0), axis=1, keepdims=True)
    high = jnp.sum(jnp.where(lane16 < 64, 0.0, prod), axis=1, keepdims=True)
    to_low = jnp.where(row16 < 9, C + 3 * row16, C + 3 * (row16 - 9) + 2)
    to_low = jnp.where(row16 == 13, C + 26, jnp.where(row16 > 13, -1, to_low))
    to_high = jnp.where(row16 < 9, C + 3 * row16 + 1, C + 3 * (row16 - 5) + 2)
    to_high = jnp.where(row16 > 12, -1, to_high)
    taps_row = jnp.where(lane16 == to_low, low, 0.0) + jnp.where(lane16 == to_high, high, 0.0)
    taps_row = jnp.sum(taps_row, axis=0, keepdims=True)
    lane = iota((1, W), 1)
    ones_row = jnp.where((lane >= 64) & (lane < 91), stats[14:15], 0.0)
    taps_row = taps_row + chosen_bias * pltpu.roll(ones_row, W - 32, 1)
    hidden_sum = jnp.sum(jnp.where(lane == 91, stats[14:15], 0.0), axis=1, keepdims=True)
    pair = pltpu.roll(stats[13:14], 64, 1)[:, 0:64]
    point = dot_high(pair, jnp.concatenate([whiten, symmetric], axis=0)) + hidden_sum * d_first
    point = jnp.concatenate([point, jnp.zeros((1, W - C), F32)], axis=1)
    row = (taps_row + point) * (1.0 / math.sqrt(count))
    row_ref[...] = jnp.broadcast_to(row, (C, W))


def grads_kernel(place_ref, left_ref, shift_ref, near_in_ref, near_ref, inner_ref, far_ref, far_in_ref,
                 dk_ref, white_ref, dvol_ref, coarse_ref, fine_ref, out_ref):
    zeros = jnp.zeros((D + 2, C, W), BF16)
    for ref in (coarse_ref, fine_ref):
        ref[:, :, 0:W] = zeros
        ref[:, :, PW - W : PW] = zeros
    inside_lo = place_ref[1].astype(F32)
    inside_hi = place_ref[2].astype(F32)
    left = left_ref[...]
    bias = shift_ref[0:C, 0:1]
    minus_offset = shift_ref[C : 2 * C, 0:1]
    even = lax.rem(lax.axis_index("space"), 2) == 0
    planes = [
        lambda: jnp.where(even, far_in_ref[...], near_in_ref[...]),
        lambda: jnp.where(even, far_ref[...], near_ref[...]),
        lambda: inner_ref[0],
        lambda: inner_ref[1],
        lambda: jnp.where(even, near_ref[...], far_ref[...]),
        lambda: jnp.where(even, near_in_ref[...], far_in_ref[...]),
    ]
    for p in range(D + 2):
        cells = planes[p]()
        both = dot(left, jnp.concatenate([cells, cells], axis=0))
        d_hidden = both[0:C] + bias
        if p == 0:
            d_hidden = d_hidden * inside_lo
        elif p > D:
            d_hidden = d_hidden * inside_hi
        else:
            white = (both[C : 2 * C] + minus_offset).astype(BF16)
            white_ref[:, p - 1] = white.reshape(C, H, W)
        terms = two_terms(d_hidden)
        coarse_ref[p, :, W : W + HW] = terms[0]
        fine_ref[p, :, W : W + HW] = terms[1]
    matrix, last_taps = tap_matrices(dk_ref, True)
    terms = two_terms(matrix)
    matrix = jnp.concatenate(terms, axis=0)
    for z in range(D):
        for start in range(0, HW, SPAN):
            coarse = offsets([coarse_ref.at[z + a] for a in range(3)], start, SPAN)
            fine = offsets([fine_ref.at[z + a] for a in range(3)], start, SPAN)
            both = dot(matrix, jnp.concatenate(coarse[:8], axis=0))
            rest = dot(terms[0], jnp.concatenate(fine[:8], axis=0))
            last = coarse[8].astype(F32) + fine[8].astype(F32)
            rows = stencil_rows(both[:96] + both[96:] + rest, last, last_taps)
            out_ref[:, start : start + SPAN] = rows.astype(BF16)
        dvol_ref[:, z] = out_ref[...].reshape(C, H, W)


def finish_kernel(rows_ref, point_ref, taps_ref):
    rows = rows_ref[...]
    point_ref[...] = rows[:, 0:C].T
    taps_ref[...] = rows[:, C : C + 27]


def cost(us):
    return pl.CostEstimate(flops=int(us * 1e8), bytes_accessed=int(us * 1e6), transcendentals=0)


def whole_step(volumes, depth_kernel, point_weight, cotangent):
    x = volumes[0]
    g = cotangent[0]
    samples = lax.axis_size("sample")
    slabs = lax.axis_size("space")
    count = float(D * HW * samples * slabs)
    scratch = [pltpu.VMEM((2, C, HW), BF16), pltpu.VMEM((208, HW), BF16)]
    vmem = pl.BlockSpec(memory_space=pltpu.VMEM)
    smem = pl.BlockSpec(memory_space=pltpu.SMEM)
    shape = jax.ShapeDtypeStruct
    near = lambda array: pltpu.with_memory_space_constraint(array, pltpu.VMEM)

    near_plane, far_plane = pl.pallas_call(
        edges_kernel,
        in_specs=[pl.BlockSpec(memory_space=pl.ANY)],
        out_shape=(pltpu.VMEM((C, H, W), BF16), pltpu.VMEM((C, H, W), BF16)),
        scratch_shapes=[pltpu.SemaphoreType.DMA((8,))],
        name="edges",
    )(x)
    partners = [(i, i ^ 1) for i in range(slabs) if i ^ 1 < slabs]
    others = [(i, i + 1 if i % 2 else i - 1) for i in range(1, slabs) if i % 2 == 0 or i + 1 < slabs]
    near_plane = lax.ppermute(near_plane, "space", partners)
    far_plane = lax.ppermute(far_plane, "space", others)
    gm_inner, acc, own, edge, matrix, last = pl.pallas_call(
        inner_kernel,
        out_shape=(
            pltpu.VMEM((2, 2 * C, HW), BF16),
            pltpu.VMEM((368, 256), F32),
            pltpu.VMEM((D, C, PW), BF16),
            pltpu.VMEM((2, C, HW), BF16),
            pltpu.VMEM((6 * C, 8 * C), BF16),
            pltpu.VMEM((3, C, W), F32),
        ),
        scratch_shapes=scratch,
        cost_estimate=cost(6),
        name="inner",
    )(x, g, depth_kernel, point_weight)
    scratch = [pltpu.VMEM((3, C, PW), BF16), pltpu.VMEM((1, C, HW), BF16), scratch[1]]
    gm_near, acc = pl.pallas_call(
        near_kernel,
        out_shape=(pltpu.VMEM((2 * C, HW), BF16), pltpu.VMEM((368, 256), F32)),
        scratch_shapes=scratch,
        cost_estimate=cost(3),
        compiler_params=pltpu.CompilerParams(vmem_limit_bytes=48 << 20),
        name="near",
    )(
        near(own), near(edge), near(near_plane), near(matrix), near(last), point_weight, near(acc)
    )
    gm_far, send = pl.pallas_call(
        far_kernel,
        out_shape=(pltpu.VMEM((2 * C, HW), BF16), pltpu.VMEM((C * ROWS, W), F32)),
        scratch_shapes=[pltpu.VMEM((368, 256), F32)] + scratch,
        cost_estimate=cost(3),
        compiler_params=pltpu.CompilerParams(vmem_limit_bytes=48 << 20),
        name="far",
    )(
        near(own), near(edge), near(far_plane), near(matrix), near(last), point_weight, near(acc)
    )
    near_in = lax.ppermute(gm_near, "space", partners)
    far_in = lax.ppermute(gm_far, "space", others)
    parts = lax.all_to_all(send.reshape(C, ROWS, W), "sample", 0, 0)
    part = jnp.broadcast_to(jnp.sum(parts, axis=0), (slabs, ROWS, W))
    pay = lax.all_to_all(part, "space", 0, 0)
    slab = lax.axis_index("space")
    place = jnp.stack([
        lax.axis_index("sample"),
        (slab > 0).astype(jnp.int32),
        (slab < slabs - 1).astype(jnp.int32),
    ])
    left, shift, row = pl.pallas_call(
        lambda *refs: terms_kernel(count, *refs),
        in_specs=[smem] + [vmem] * 2,
        out_shape=(
            pltpu.VMEM((2 * C, 4 * C), BF16),
            pltpu.VMEM((2 * C, W), F32),
            pltpu.VMEM((C, W), F32),
        ),
        cost_estimate=cost(4),
        name="terms",
    )(place, near(pay), point_weight)
    rows = lax.all_to_all(row.reshape(C, 1, W), "sample", 0, 0).reshape(C, W)
    white, d_volume = pl.pallas_call(
        grads_kernel,
        in_specs=[smem] + [vmem] * 8,
        out_shape=(shape((C, D, H, W), BF16), shape((C, D, H, W), BF16)),
        scratch_shapes=[
            pltpu.VMEM((D + 2, C, PW), BF16),
            pltpu.VMEM((D + 2, C, PW), BF16),
            pltpu.VMEM((C, HW), BF16),
        ],
        cost_estimate=cost(8),
        name="grads",
    )(
        place, near(left), near(shift), near(near_in), near(gm_near), near(gm_inner),
        near(gm_far), near(far_in), depth_kernel,
    )
    d_point, d_kernel = pl.pallas_call(
        finish_kernel,
        out_shape=(shape((C, C), F32), shape((C, 27), F32)),
        in_specs=[vmem],
        name="finish",
    )(near(rows))
    return white[None], d_volume[None], d_point, d_kernel


def solution(mesh):
    split = P("sample", None, "space", None, None)
    return jax.shard_map(
        whole_step,
        mesh=mesh,
        in_specs=(split, P(), P(), split),
        out_specs=(split, split, P(), P()),
        check_vma=False,
    )
```
